32 devices in a mesh: band: 4 (over y, x), slab: 8 (over z, core).
Axes of the slice: x: 2, y: 2, z: 4, core: 2. Of those that a mesh axis runs over, the one named last changes fastest.
Arguments:
- coefficients: float32 [8, 96, 96, 192], P('band', 'slab'), may hold values from -6 to 6
- occupation: int32 [8], P('band'), may hold values from 1 to 2
- pencil_reach: int32 [96, 96], P('slab'), may hold values from -1 to 47
- external: float32 [192, 192, 192], P(None, 'slab'), may hold values from -3 to 3
Outputs:
- applied: float32 [8, 96, 96, 192], P('band', 'slab')
- potential: float32 [192, 192, 192], P(None, 'slab')
The draws below stay inside these ranges and needn't reach their ends.
All inputs are finite; a program needn't handle non-finite values.
Results may differ from the reference program's by a relative error of at most 0.00011.
Values sent between devices are 32-bit elements; how exact they have to be, the bound alone decides.
A program may use at most 128 MiB of HBM per device.

```python
import jax
import jax.numpy as jnp
from jax import lax

NW = 96
NG = 192
BANDS = 8


def draw_pencil_reach(key, part):
    halfway = NW // 2
    key_radius = jax.random.fold_in(key, 11)
    key_jitter = jax.random.fold_in(key, 23)
    radius_sq = jax.random.randint(key_radius, (), (halfway - 1) * (halfway - 1), halfway * halfway, dtype=jnp.int32)
    indices = jnp.arange(NW, dtype=jnp.int32)
    frequencies = jnp.where(indices < halfway, indices, indices - NW)
    planar = frequencies[:, None] * frequencies[:, None] + frequencies[None, :] * frequencies[None, :]
    offsets = jnp.arange(halfway + 1, dtype=jnp.int32)
    inside = planar[:, :, None] + offsets[None, None, :] * offsets[None, None, :] <= radius_sq
    extent = jnp.sum(inside.astype(jnp.int32), axis=2) - 1
    jitter = jax.random.randint(key_jitter, (NW, NW), 0, 2, dtype=jnp.int32)
    jitter = jnp.where(planar == 0, 0, jitter)
    return jnp.maximum(extent - jitter, -1)


def place_ends(values, key, smallest, largest):
    shape = values.shape
    index_at = [jax.random.randint(jax.random.fold_in(key, axis), (), 0, shape[axis]) for axis in range(len(shape))]
    values = values.at[tuple(index_at)].set(smallest)
    longest = shape.index(max(shape))
    index_at[longest] = (index_at[longest] + 1) % shape[longest]
    return values.at[tuple(index_at)].set(largest)


def block_levels(rng, dims, shards, least, high):
    level, own = 1.0, jax.random.fold_in(rng, 6)
    for dim, shards_of in shards:
        heights = jnp.exp(jax.random.uniform(jax.random.fold_in(own, dim), (shards_of,), jnp.float32, least / len(shards), high / len(shards)))
        level = level * jnp.repeat(heights, dims[dim] // shards_of).reshape([-1 if axis == dim else 1 for axis in range(len(dims))])
    return level


def centred(key, shape, deviation, most, shards=(), kind=jnp.bfloat16):
    result = jax.random.normal(key, shape, jnp.float32) * deviation
    if len(shards) > 0:
        result = block_levels(key, shape, shards, -0.22, 0.18) * result
    return jnp.clip(result, min=-most, max=most).astype(kind)


def setup_inputs(seed: int = 0) -> dict:
    keys = jax.random.split(jax.random.key(seed), 5)
    coefficients = centred(keys[0], (BANDS, NW, NW, 2 * NW), 1.0, 6.0, ((0, 4), (1, 8)), jnp.float32)
    occupation = place_ends(jax.random.randint(keys[1], (BANDS,), 1, 3), jax.random.fold_in(keys[1], 1), 1, 2).astype(jnp.int32)
    pencil_reach = draw_pencil_reach(jax.random.fold_in(keys[4], 71), 0)
    external = centred(keys[3], (NG, NG, NG), 0.5, 3.0, ((1, 8),), jnp.float32)
    return dict(coefficients=coefficients, occupation=occupation, pencil_reach=pencil_reach, external=external)


KINETIC = 0.0005
SLATER = 0.9847


def frequency(length):
    indices = jnp.arange(length, dtype=jnp.int32)
    return jnp.where(indices < length // 2, indices, indices - length)


def embed_grid(values):
    halfway = NW // 2
    for dimension in range(3):
        lower = lax.slice_in_dim(values, 0, halfway, axis=dimension)
        upper = lax.slice_in_dim(values, halfway, NW, axis=dimension)
        padding_shape = list(values.shape)
        padding_shape[dimension] = NG - NW
        values = jnp.concatenate([lower, jnp.zeros(padding_shape, values.dtype), upper], axis=dimension)
    return values


def extract_grid(values):
    halfway = NW // 2
    for dimension in range(3):
        lower = lax.slice_in_dim(values, 0, halfway, axis=dimension)
        upper = lax.slice_in_dim(values, NG - halfway, NG, axis=dimension)
        values = jnp.concatenate([lower, upper], axis=dimension)
    return values


def to_real(coefficient, sphere):
    real_part = coefficient[..., :NW] * sphere
    imag_part = coefficient[..., NW:] * sphere
    spectrum = lax.complex(real_part, imag_part)
    return jnp.fft.ifftn(embed_grid(spectrum)) * (NG ** 3 / NW ** 1.5)


def reference(coefficients, occupation, pencil_reach, external):
    wavenumbers = frequency(NW)
    sphere = (jnp.abs(wavenumbers)[None, None, :] <= pencil_reach[:, :, None]).astype(jnp.float32)
    weights = occupation.astype(jnp.float32) / BANDS

    def add_band(running, members):
        coefficient, weight = members
        wavefield = to_real(coefficient, sphere)
        squares = jnp.real(wavefield) * jnp.real(wavefield) + jnp.imag(wavefield) * jnp.imag(wavefield)
        return running + weight * squares, None

    density, _ = lax.scan(add_band, jnp.zeros((NG, NG, NG), jnp.float32), (coefficients, weights))
    potential_xyz = jnp.transpose(external, (0, 2, 1)) - SLATER * jnp.cbrt(density)
    squared = (wavenumbers * wavenumbers).astype(jnp.float32)
    kinetic = KINETIC * (squared[:, None, None] + squared[None, :, None] + squared[None, None, :])

    def apply_band(coefficient):
        wavefield = to_real(coefficient, sphere)
        returned = extract_grid(jnp.fft.fftn(wavefield * potential_xyz)) * (NW ** 1.5 / NG ** 3)
        real_out = sphere * (kinetic * (coefficient[..., :NW] * sphere) + jnp.real(returned))
        imag_out = sphere * (kinetic * (coefficient[..., NW:] * sphere) + jnp.imag(returned))
        return jnp.concatenate([real_out, imag_out], axis=-1)

    applied = lax.map(apply_band, coefficients)
    return applied, jnp.transpose(potential_xyz, (0, 2, 1))
```

```python
import functools
import math

import jax
import jax.numpy as jnp
import ml_dtypes
import numpy as np
from jax import lax
from jax.experimental import pallas as pl
from jax.experimental.pallas import tpu as pltpu
from jax.sharding import PartitionSpec as P

KINETIC = 0.0005
SLATER = 0.9847
COUNT = 2
MESH = pl.DeviceIdType.MESH


def frequency(length):
    indices = jnp.arange(length, dtype=jnp.int32)
    return jnp.where(indices < length // 2, indices, indices - length)


def inverse_table(length, extent):
    wavenumbers = frequency(length)
    positions = jnp.arange(extent, dtype=jnp.int32)
    phases = positions[:, None] * wavenumbers[None, :] % extent
    angles = phases.astype(jnp.float32) * (2.0 * math.pi / extent)
    factor = length ** (-0.5)
    cosine = jnp.cos(angles) * factor
    sine_part = jnp.sin(angles) * factor
    return jnp.stack([jnp.stack([cosine, -sine_part], 1), jnp.stack([sine_part, cosine], 1)], 0)


def forward_table(length, extent):
    wavenumbers = frequency(length)
    positions = jnp.arange(extent, dtype=jnp.int32)
    phases = wavenumbers[:, None] * positions[None, :] % extent
    angles = phases.astype(jnp.float32) * (2.0 * math.pi / extent)
    factor = length**0.5 / extent
    cosine = jnp.cos(angles) * factor
    sine_part = jnp.sin(angles) * factor
    return jnp.stack([jnp.stack([cosine, sine_part], 1), jnp.stack([-sine_part, cosine], 1)], 0)


def contract(form, left, right):
    return jnp.einsum(form, left, right, precision=lax.Precision.HIGH)


def slab_plan(coefficients, occupation, pencil_reach, external):
    nbands, planes, width, doubled = coefficients.shape
    points = 2 * width
    slabs = lax.axis_size("slab")
    layers = points // slabs
    groups = lax.axis_size("band")
    inverse = inverse_table(width, points)
    forward = forward_table(width, points)
    wavenumbers = frequency(width)
    sphere = (jnp.abs(wavenumbers)[None, None, :] <= pencil_reach[:, :, None]).astype(jnp.float32)
    sphere_full = sphere[None, :, :, None, :]
    masked = coefficients.reshape(nbands, planes, width, 2, width) * sphere_full
    along_z = contract("bxgci,onci->bxnog", masked, inverse)
    flattened = along_z.reshape(nbands, planes, points, 2 * width)
    received = lax.all_to_all(flattened, "slab", split_axis=2, concat_axis=1, tiled=True)
    columns = received.reshape(received.shape[0], width, layers, 2, width)
    spread = contract("bkzcg,oycg->bkzoy", columns, inverse)
    wavefield = contract("bkzcy,oxck->bxzoy", spread, inverse)
    squares = jnp.sum(wavefield * wavefield, axis=3)
    weights = occupation.astype(jnp.float32) / (nbands * groups)
    partial_value = contract("b,bxzy->xzy", weights, squares)
    rows_all = points * layers
    share = (rows_all + groups - 1) // groups
    flat_partial = partial_value.reshape(rows_all, points)
    density = lax.psum_scatter(flat_partial, "band", scatter_dimension=0, tiled=True)
    flat_external = external.reshape(rows_all, points)
    start_row = lax.axis_index("band") * share
    own_external = lax.dynamic_slice_in_dim(flat_external, start_row, share, 0)
    own_potential = own_external - SLATER * jnp.cbrt(density)
    gathered = lax.all_gather(own_potential, "band", axis=0, tiled=True)
    potential_all = gathered.reshape(points, layers, points)
    product = wavefield * potential_all[None, :, :, None, :]
    back_rows = contract("bxzcy,okcx->bkzoy", product, forward)
    back_y = contract("bkzcy,ogcy->bkzog", back_rows, forward).reshape(
        nbands, width, layers, 2 * width
    )
    received = lax.all_to_all(back_y, "slab", split_axis=1, concat_axis=2, tiled=True)
    blocks = received.reshape(received.shape[0], planes, points, 2, width)
    returned = contract("bxncg,ohcn->bxgoh", blocks, forward)
    plane_index = lax.axis_index("slab") * planes + jnp.arange(planes, dtype=jnp.int32)
    plane_freq = jnp.where(plane_index < width // 2, plane_index, plane_index - width)
    plane_sq = (plane_freq * plane_freq).astype(jnp.float32)
    wave_sq = (wavenumbers * wavenumbers).astype(jnp.float32)
    kinetic = KINETIC * (plane_sq[:, None, None] + wave_sq[None, :, None] + wave_sq[None, None, :])
    finished = sphere_full * (kinetic[None, :, :, None, :] * masked + returned)
    return (finished.reshape(nbands, planes, width, 2 * width), potential_all)


def split_np(table):
    high = table.astype(ml_dtypes.bfloat16)
    low = (table - high.astype(np.float64)).astype(ml_dtypes.bfloat16)
    return high, low


def split(value):
    high = value.astype(jnp.bfloat16)
    low = (value - high.astype(jnp.float32)).astype(jnp.bfloat16)
    return high, low


def dot(left, right):
    return jnp.dot(left, right, preferred_element_type=jnp.float32)


def dot_t(left, right):
    return lax.dot_general(left, right, (((1,), (1,)), ((), ())), preferred_element_type=jnp.float32)


def fused_tables(width, nbands, planes, slabs, groups, own):
    points = 2 * width
    doubled = 2 * width
    layers = points // slabs
    chunks = own // COUNT
    rows = COUNT * planes
    indices = np.arange(width)
    wave = np.where(indices < width // 2, indices, indices - width)
    phase = (np.arange(points)[:, None] * wave[None, :]) % points
    angles = phase * (2.0 * math.pi / points)
    cos, sin = np.cos(angles), np.sin(angles)
    inv = width**-0.5
    fwd = width**0.5 / points
    z_of = np.array(
        [
            [
                s * layers + g * own + part * COUNT + p
                for p in range(COUNT)
                for g in range(groups)
                for s in range(slabs)
            ]
            for part in range(chunks)
        ]
    )
    tz = np.concatenate([cos, -sin], 1)[z_of] * inv
    span = doubled + 64
    ty = np.zeros((nbands, 2, span, points))
    tyb = np.zeros((nbands, 2, points, span))
    for b in range(nbands):
        shift = b * doubled - b * 128
        ty[b, 0, shift:shift + width] = cos.T * inv
        ty[b, 0, shift + width:shift + doubled] = -sin.T * inv
        ty[b, 1, shift:shift + width] = sin.T * inv
        ty[b, 1, shift + width:shift + doubled] = cos.T * inv
        tyb[b, 0, :, shift:shift + width] = cos * fwd
        tyb[b, 0, :, shift + width:shift + doubled] = -sin * fwd
        tyb[b, 1, :, shift:shift + width] = sin * fwd
        tyb[b, 1, :, shift + width:shift + doubled] = cos * fwd
    window = 16
    tx = np.zeros((COUNT, 2, points, 2, slabs, window))
    txb = np.zeros((COUNT, 2, slabs, window, 2, points))
    for p in range(COUNT):
        first = p * planes - p * (rows - window)
        put = slice(first, first + planes)
        c3 = cos.reshape(points, slabs, planes)
        s3 = sin.reshape(points, slabs, planes)
        tx[p, 0, :, 0][:, :, put] = c3 * inv
        tx[p, 0, :, 1][:, :, put] = -s3 * inv
        tx[p, 1, :, 0][:, :, put] = s3 * inv
        tx[p, 1, :, 1][:, :, put] = c3 * inv
        ct, st = c3.transpose(1, 2, 0), s3.transpose(1, 2, 0)
        txb[p, 0][:, put, 0] = ct * fwd
        txb[p, 0][:, put, 1] = st * fwd
        txb[p, 1][:, put, 0] = -st * fwd
        txb[p, 1][:, put, 1] = ct * fwd
    tx = tx.reshape(COUNT, 2 * points, 2 * slabs * window)
    txb = txb.reshape(COUNT, 2 * slabs * window, 2 * points)
    tzb = np.stack([np.concatenate([cos, -sin], 1)[z_of], np.concatenate([sin, cos], 1)[z_of]], 1) * fwd
    return tz, ty, tx, txb, tyb, tzb


def fused_kernel(
    sizes,
    coef, reach, absk, occ, ext, kin,
    tzh, tzl, tyh, tyl, txh, txl, txbh, txbl, tybh, tybl, tzbh, tzbl,
    out, vall,
    xh, xl, send, recv, sendb, recvb, wave, dens, weights,
    send_sem, recv_sem, sendb_sem, recvb_sem, v_send, v_recv, w_send, w_recv,
):
    nbands, planes, width, slabs, groups, own = sizes
    points = 2 * width
    doubled = 2 * width
    chunks = own // COUNT
    members = groups * slabs
    rows = COUNT * planes
    block = slabs * rows
    tiles = nbands * doubled // 128
    window = 16
    group = lax.axis_index("band")
    slab = lax.axis_index("slab")
    me = group * slabs + slab

    barrier = pltpu.get_barrier_semaphore()

    def greet(step, carry):
        other = lax.rem(me + step, members)
        pl.semaphore_signal(barrier, inc=1, device_id=(other // slabs, lax.rem(other, slabs)), device_id_type=MESH)
        return carry

    lax.fori_loop(1, members, greet, 0)

    def at_block(ref, chunk, member):
        return ref.at[chunk, pl.ds(pl.multiple_of(member * tiles * rows, 8), tiles * rows), :]

    def prepare(gx, carry):
        pieces = []
        keep = absk[...] <= reach[gx]
        for b in range(nbands):
            value = jnp.where(keep, coef[b, gx], 0.0)
            pieces.append(value)
            pieces.append(jnp.concatenate([value[:, width:], -value[:, :width]], axis=1))
        high, low = split(jnp.concatenate(pieces, axis=0))
        xh[gx] = high
        xl[gx] = low
        return carry

    lax.fori_loop(0, planes, prepare, 0)

    def z_spread(chunk):
        def one(gx, carry):
            high, low = xh[gx], xl[gx]
            value = dot_t(tzh[chunk], high) + dot_t(tzl[chunk], high) + dot_t(tzh[chunk], low)
            for p in range(COUNT):
                for tile in range(tiles):
                    start = tile * rows + p * planes + gx
                    piece = value[p * members:(p + 1) * members, tile * 128:(tile + 1) * 128]
                    send[chunk, pl.ds(start, members, stride=tiles * rows), :] = piece
            return carry

        lax.fori_loop(0, planes, one, 0)

    def other_of(step):
        turn = lax.rem(step + slabs // 2, slabs)
        return lax.rem(group + step // slabs, groups), lax.rem(slab + turn, slabs)

    def push(chunk, from_ref, to_ref, sems, rsems, tgroup, tslab):
        pltpu.make_async_remote_copy(
            src_ref=at_block(from_ref, chunk, tgroup * slabs + tslab),
            dst_ref=at_block(to_ref, chunk, me),
            send_sem=sems.at[chunk],
            recv_sem=rsems.at[chunk],
            device_id=(tgroup, tslab),
            device_id_type=MESH,
        ).start()

    def keep_own(chunk, from_ref, to_ref, rsems):
        pltpu.make_async_copy(at_block(from_ref, chunk, me), at_block(to_ref, chunk, me), rsems.at[chunk]).start()

    def spread_out(chunk):
        z_spread(chunk)

        def one(step, carry):
            tgroup, tslab = other_of(step)

            @pl.when(tgroup * slabs + tslab != me)
            def _():
                push(chunk, send, recv, send_sem, recv_sem, tgroup, tslab)

            return carry

        lax.fori_loop(0, members, one, 0)
        keep_own(chunk, send, recv, recv_sem)

    def wait_all(ref, sems, chunk):
        pltpu.make_async_copy(ref.at[chunk], ref.at[chunk], sems.at[chunk]).wait()

    def share_planes(step, ref_at, send_at, recv_at):
        tgroup = lax.rem(group + step, groups)
        pltpu.make_async_remote_copy(
            src_ref=ref_at, dst_ref=ref_at, send_sem=send_at, recv_sem=recv_at,
            device_id=(tgroup, slab), device_id_type=MESH,
        ).start()

    pl.semaphore_wait(barrier, members - 1)

    weights[group] = occ[...]
    for step in range(1, groups):
        share_planes(step, weights.at[group], w_send.at[0], w_recv.at[0])

    for chunk in range(chunks):
        spread_out(chunk)

    others = weights.at[pl.ds(0, groups - 1)]
    pltpu.make_async_copy(others, others, w_recv.at[0]).wait()
    pltpu.make_async_copy(others, others, w_send.at[0]).wait()

    def middle(chunk, carry):
        wait_all(recv, recv_sem, chunk)
        dens[...] = jnp.zeros_like(dens)

        def build(g, carry):
            arrived = recv[chunk, pl.ds(pl.multiple_of(g * tiles * block, 8), tiles * block), :]
            arrived = arrived.reshape(slabs, tiles, rows, 128)
            high, low = split(
                jnp.concatenate([arrived[:, tile].reshape(block, 128) for tile in range(tiles)], axis=1)
            )
            for b in range(nbands):
                first = b * 128
                lh = high[:, first:first + doubled + 64]
                ll = low[:, first:first + doubled + 64]
                parts = []
                for c in range(2):
                    y = dot(lh, tyh[b, c]) + dot(lh, tyl[b, c]) + dot(ll, tyh[b, c])
                    parts.append(y.reshape(slabs, rows, points))
                w = weights[g, b, 0:1, 0:1]
                for p in range(COUNT):
                    lead = p * (rows - window)
                    stacked = jnp.concatenate(
                        [part[:, lead:lead + window].reshape(slabs * window, points) for part in parts], axis=0
                    )
                    yh, yl = split(stacked)
                    field = dot(txh[p], yh) + dot(txl[p], yh) + dot(txh[p], yl)
                    wave[p, g * nbands + b] = field
                    dens[p] += w * (field[:points] * field[:points] + field[points:] * field[points:])
            return carry

        lax.fori_loop(0, groups, build, 0)
        potentials = []
        for p in range(COUNT):
            d = dens[p]
            potential = ext[chunk * COUNT + p] - SLATER * jnp.exp(jnp.log(d) * (1.0 / 3.0))
            potentials.append(potential)
            dens[p] = potential
        vall[group, chunk] = jnp.concatenate(potentials, axis=1)
        for step in range(1, groups):
            share_planes(step, vall.at[group, chunk], v_send.at[0], v_recv.at[0])

        def back(turn, carry):
            g = lax.rem(group + turn, groups)
            sums = []
            for b in range(nbands):
                boths = []
                for p in range(COUNT):
                    potential = dens[p]
                    field = wave[p, g * nbands + b]
                    product = jnp.concatenate([field[:points] * potential, field[points:] * potential], axis=0)
                    ph, pll = split(product)
                    boths.append(dot(txbh[p], ph) + dot(txbl[p], ph) + dot(txbh[p], pll))
                total = None
                for c in range(2):
                    low_rows, high_rows = [
                        both[c * slabs * window:(c + 1) * slabs * window].reshape(slabs, window, points) for both in boths
                    ]
                    cut = rows - window
                    merged = jnp.concatenate(
                        [low_rows[:, :cut], low_rows[:, cut:] + high_rows[:, :window - cut], high_rows[:, window - cut:]], axis=1
                    ).reshape(block, points)
                    mh, ml = split(merged)
                    value = dot(mh, tybh[b, c]) + dot(mh, tybl[b, c]) + dot(ml, tybh[b, c])
                    total = value if total is None else total + value
                sums.append(total)
            first, second = sums
            pieces = [first[:, :128], first[:, 128:] + second[:, :128], second[:, 128:]]
            sendb[chunk, pl.ds(pl.multiple_of(g * tiles * block, 8), tiles * block), :] = jnp.concatenate(
                [piece.reshape(slabs, 1, rows, 128) for piece in pieces], axis=1
            ).reshape(tiles * block, 128)

            def one(step, carry):
                tslab = lax.rem(slab + step + slabs // 2, slabs)

                @pl.when(g * slabs + tslab != me)
                def _():
                    push(chunk, sendb, recvb, sendb_sem, recvb_sem, g, tslab)

                return carry

            lax.fori_loop(0, slabs, one, 0)
            return carry

        lax.fori_loop(0, groups, back, 0)
        keep_own(chunk, sendb, recvb, recvb_sem)
        return carry

    lax.fori_loop(0, chunks, middle, 0)

    def z_back(chunk):
        wait_all(recvb, recvb_sem, chunk)

        def one(gx, carry):
            columns = []
            for tile in range(tiles):
                starts = [tile * rows + p * planes + gx for p in range(COUNT)]
                columns.append(jnp.concatenate(
                    [recvb[chunk, pl.ds(start, members, stride=tiles * rows), :] for start in starts], axis=0
                ))
            turned = jnp.concatenate(columns, axis=1).T
            high, low = split(turned)
            for b in range(nbands):
                total = None
                for c in range(2):
                    first = (b * 2 + c) * width
                    th, tl = high[first:first + width], low[first:first + width]
                    part = dot(th, tzbh[chunk, c]) + dot(th, tzbl[chunk, c]) + dot(tl, tzbh[chunk, c])
                    total = part if total is None else total + part
                if chunk > 0:
                    total = total + out[b, gx]
                if chunk == chunks - 1:
                    keep = absk[...] <= reach[gx]
                    total = jnp.where(keep, kin[gx] * coef[b, gx] + total, 0.0)
                out[b, gx] = total
            return carry

        lax.fori_loop(0, planes, one, 0)

    for chunk in range(chunks):
        z_back(chunk)

    def wait_sent(ref, sems, chunk):
        sent = ref.at[chunk, pl.ds(0, (members - 1) * tiles * rows), :]
        pltpu.make_async_copy(sent, sent, sems.at[chunk]).wait()

    for chunk in range(chunks):
        wait_sent(send, send_sem, chunk)
        wait_sent(sendb, sendb_sem, chunk)
    given = vall.at[pl.ds(0, groups - 1)]
    pltpu.make_async_copy(given, given, v_send.at[0]).wait()
    pltpu.make_async_copy(given, given, v_recv.at[0]).wait()


def fused_plan(coefficients, occupation, pencil_reach, external):
    nbands, planes, width, doubled = coefficients.shape
    points = 2 * width
    slabs = lax.axis_size("slab")
    groups = lax.axis_size("band")
    layers = points // slabs
    own = layers // groups
    chunks = own // COUNT
    members = groups * slabs
    rows = COUNT * planes
    lanes = nbands * doubled
    group = lax.axis_index("band")
    tables = []
    for table in fused_tables(width, nbands, planes, slabs, groups, own):
        high, low = split_np(table)
        tables += [jnp.asarray(high), jnp.asarray(low)]
    wavenumbers = np.where(np.arange(width) < width // 2, np.arange(width), np.arange(width) - width)
    absk = jnp.asarray(np.abs(np.concatenate([wavenumbers, wavenumbers]))[None].astype(np.int32))
    reach = pencil_reach[:, :, None]
    weights = occupation.astype(jnp.float32) / (nbands * groups)
    occ = jnp.broadcast_to(weights[:, None, None], (nbands, 8, 128))
    ext = lax.dynamic_slice_in_dim(external, group * own, own, 1).transpose(1, 0, 2)
    plane_index = lax.axis_index("slab") * planes + jnp.arange(planes, dtype=jnp.int32)
    plane_freq = jnp.where(plane_index < width // 2, plane_index, plane_index - width)
    plane_sq = (plane_freq * plane_freq).astype(jnp.float32)
    square = (wavenumbers * wavenumbers).astype(np.float32)
    twice = np.concatenate([square, square])
    kin = KINETIC * (plane_sq[:, None, None] + square[None, :, None] + twice[None, None, :])
    vmem = pl.BlockSpec(memory_space=pltpu.VMEM)
    operands = [coefficients, reach, absk, occ, ext, kin] + tables
    bf, f32 = jnp.bfloat16, jnp.float32
    dma = pltpu.SemaphoreType.DMA
    applied, vall = pl.pallas_call(
        functools.partial(fused_kernel, (nbands, planes, width, slabs, groups, own)),
        name="fused",
        out_shape=[
            jax.ShapeDtypeStruct(coefficients.shape, f32),
            jax.ShapeDtypeStruct((groups, chunks, points, COUNT * points), f32),
        ],
        in_specs=[vmem] * len(operands),
        out_specs=[vmem, vmem],
        scratch_shapes=[
            pltpu.VMEM((planes, nbands * 2 * width, doubled), bf),
            pltpu.VMEM((planes, nbands * 2 * width, doubled), bf),
            pltpu.VMEM((chunks, members * rows * lanes // 128, 128), f32),
            pltpu.VMEM((chunks, members * rows * lanes // 128, 128), f32),
            pltpu.VMEM((chunks, members * rows * lanes // 128, 128), f32),
            pltpu.VMEM((chunks, members * rows * lanes // 128, 128), f32),
            pltpu.VMEM((COUNT, groups * nbands, 2 * points, points), f32),
            pltpu.VMEM((COUNT, points, points), f32),
            pltpu.VMEM((groups, nbands, 8, 128), f32),
            dma((chunks,)), dma((chunks,)), dma((chunks,)), dma((chunks,)),
            dma((1,)), dma((1,)), dma((1,)), dma((1,)),
        ],
        compiler_params=pltpu.CompilerParams(
            collective_id=0, has_side_effects=True, vmem_limit_bytes=58 * 2**20
        ),
    )(*operands)
    potential = vall.reshape(groups, chunks, points, COUNT, points).transpose(2, 0, 1, 3, 4)
    return applied, potential.reshape(points, layers, points)


def shards(coefficients, occupation, pencil_reach, external):
    nbands, planes, width, doubled = coefficients.shape
    slabs, groups = lax.axis_size("slab"), lax.axis_size("band")
    layers = doubled // slabs
    fits = (
        layers % (groups * COUNT) == 0 and nbands == 2 and planes == 12 and width == 96 and COUNT == 2
    )
    plan = fused_plan if fits else slab_plan
    return plan(coefficients, occupation, pencil_reach, external)


def solution(mesh):
    return jax.shard_map(
        shards,
        mesh=mesh,
        in_specs=(P("band", "slab", None, None), P("band"), P("slab", None), P(None, "slab", None)),
        out_specs=(P("band", "slab", None, None), P(None, "slab", None)),
        check_vma=False,
    )
```

```python
import functools
import math

import jax
import jax.numpy as jnp
import ml_dtypes
import numpy as np
from jax import lax
from jax.experimental import pallas as pl
from jax.experimental.pallas import tpu as pltpu
from jax.sharding import PartitionSpec as P

KINETIC = 0.0005
SLATER = 0.9847
COUNT = 2
MESH = pl.DeviceIdType.MESH


def frequency(length):
    indices = jnp.arange(length, dtype=jnp.int32)
    return jnp.where(indices < length // 2, indices, indices - length)


def inverse_table(length, extent):
    wavenumbers = frequency(length)
    positions = jnp.arange(extent, dtype=jnp.int32)
    phases = positions[:, None] * wavenumbers[None, :] % extent
    angles = phases.astype(jnp.float32) * (2.0 * math.pi / extent)
    factor = length ** (-0.5)
    cosine = jnp.cos(angles) * factor
    sine_part = jnp.sin(angles) * factor
    return jnp.stack([jnp.stack([cosine, -sine_part], 1), jnp.stack([sine_part, cosine], 1)], 0)


def forward_table(length, extent):
    wavenumbers = frequency(length)
    positions = jnp.arange(extent, dtype=jnp.int32)
    phases = wavenumbers[:, None] * positions[None, :] % extent
    angles = phases.astype(jnp.float32) * (2.0 * math.pi / extent)
    factor = length**0.5 / extent
    cosine = jnp.cos(angles) * factor
    sine_part = jnp.sin(angles) * factor
    return jnp.stack([jnp.stack([cosine, sine_part], 1), jnp.stack([-sine_part, cosine], 1)], 0)


def contract(form, left, right):
    return jnp.einsum(form, left, right, precision=lax.Precision.HIGH)


def slab_plan(coefficients, occupation, pencil_reach, external):
    nbands, planes, width, doubled = coefficients.shape
    points = 2 * width
    slabs = lax.axis_size("slab")
    layers = points // slabs
    groups = lax.axis_size("band")
    inverse = inverse_table(width, points)
    forward = forward_table(width, points)
    wavenumbers = frequency(width)
    sphere = (jnp.abs(wavenumbers)[None, None, :] <= pencil_reach[:, :, None]).astype(jnp.float32)
    sphere_full = sphere[None, :, :, None, :]
    masked = coefficients.reshape(nbands, planes, width, 2, width) * sphere_full
    along_z = contract("bxgci,onci->bxnog", masked, inverse)
    flattened = along_z.reshape(nbands, planes, points, 2 * width)
    received = lax.all_to_all(flattened, "slab", split_axis=2, concat_axis=1, tiled=True)
    columns = received.reshape(received.shape[0], width, layers, 2, width)
    spread = contract("bkzcg,oycg->bkzoy", columns, inverse)
    wavefield = contract("bkzcy,oxck->bxzoy", spread, inverse)
    squares = jnp.sum(wavefield * wavefield, axis=3)
    weights = occupation.astype(jnp.float32) / (nbands * groups)
    partial_value = contract("b,bxzy->xzy", weights, squares)
    rows_all = points * layers
    share = (rows_all + groups - 1) // groups
    flat_partial = partial_value.reshape(rows_all, points)
    density = lax.psum_scatter(flat_partial, "band", scatter_dimension=0, tiled=True)
    flat_external = external.reshape(rows_all, points)
    start_row = lax.axis_index("band") * share
    own_external = lax.dynamic_slice_in_dim(flat_external, start_row, share, 0)
    own_potential = own_external - SLATER * jnp.cbrt(density)
    gathered = lax.all_gather(own_potential, "band", axis=0, tiled=True)
    potential_all = gathered.reshape(points, layers, points)
    product = wavefield * potential_all[None, :, :, None, :]
    back_rows = contract("bxzcy,okcx->bkzoy", product, forward)
    back_y = contract("bkzcy,ogcy->bkzog", back_rows, forward).reshape(
        nbands, width, layers, 2 * width
    )
    received = lax.all_to_all(back_y, "slab", split_axis=1, concat_axis=2, tiled=True)
    blocks = received.reshape(received.shape[0], planes, points, 2, width)
    returned = contract("bxncg,ohcn->bxgoh", blocks, forward)
    plane_index = lax.axis_index("slab") * planes + jnp.arange(planes, dtype=jnp.int32)
    plane_freq = jnp.where(plane_index < width // 2, plane_index, plane_index - width)
    plane_sq = (plane_freq * plane_freq).astype(jnp.float32)
    wave_sq = (wavenumbers * wavenumbers).astype(jnp.float32)
    kinetic = KINETIC * (plane_sq[:, None, None] + wave_sq[None, :, None] + wave_sq[None, None, :])
    finished = sphere_full * (kinetic[None, :, :, None, :] * masked + returned)
    return (finished.reshape(nbands, planes, width, 2 * width), potential_all)


def split_np(table):
    high = table.astype(ml_dtypes.bfloat16)
    low = (table - high.astype(np.float64)).astype(ml_dtypes.bfloat16)
    return high, low


def split(value):
    high = value.astype(jnp.bfloat16)
    low = (value - high.astype(jnp.float32)).astype(jnp.bfloat16)
    return high, low


def dot(left, right):
    return jnp.dot(left, right, preferred_element_type=jnp.float32)


def dot_t(left, right):
    return lax.dot_general(left, right, (((1,), (1,)), ((), ())), preferred_element_type=jnp.float32)


def fused_tables(width, nbands, planes, slabs, groups, own):
    points = 2 * width
    doubled = 2 * width
    layers = points // slabs
    chunks = own // COUNT
    rows = COUNT * planes
    indices = np.arange(width)
    wave = np.where(indices < width // 2, indices, indices - width)
    phase = (np.arange(points)[:, None] * wave[None, :]) % points
    angles = phase * (2.0 * math.pi / points)
    cos, sin = np.cos(angles), np.sin(angles)
    inv = width**-0.5
    fwd = width**0.5 / points
    z_of = np.array(
        [
            [
                s * layers + g * own + part * COUNT + p
                for p in range(COUNT)
                for g in range(groups)
                for s in range(slabs)
            ]
            for part in range(chunks)
        ]
    )
    tz = np.concatenate([cos, -sin], 1)[z_of] * inv
    span = doubled + 64
    ty = np.zeros((nbands, 2, span, points))
    tyb = np.zeros((nbands, 2, points, span))
    for b in range(nbands):
        shift = b * doubled - b * 128
        ty[b, 0, shift:shift + width] = cos.T * inv
        ty[b, 0, shift + width:shift + doubled] = -sin.T * inv
        ty[b, 1, shift:shift + width] = sin.T * inv
        ty[b, 1, shift + width:shift + doubled] = cos.T * inv
        tyb[b, 0, :, shift:shift + width] = cos * fwd
        tyb[b, 0, :, shift + width:shift + doubled] = -sin * fwd
        tyb[b, 1, :, shift:shift + width] = sin * fwd
        tyb[b, 1, :, shift + width:shift + doubled] = cos * fwd
    window = 16
    tx = np.zeros((COUNT, 2, points, 2, slabs, window))
    txb = np.zeros((COUNT, 2, slabs, window, 2, points))
    for p in range(COUNT):
        first = p * planes - p * (rows - window)
        put = slice(first, first + planes)
        c3 = cos.reshape(points, slabs, planes)
        s3 = sin.reshape(points, slabs, planes)
        tx[p, 0, :, 0][:, :, put] = c3 * inv
        tx[p, 0, :, 1][:, :, put] = -s3 * inv
        tx[p, 1, :, 0][:, :, put] = s3 * inv
        tx[p, 1, :, 1][:, :, put] = c3 * inv
        ct, st = c3.transpose(1, 2, 0), s3.transpose(1, 2, 0)
        txb[p, 0][:, put, 0] = ct * fwd
        txb[p, 0][:, put, 1] = st * fwd
        txb[p, 1][:, put, 0] = -st * fwd
        txb[p, 1][:, put, 1] = ct * fwd
    tx = tx.reshape(COUNT, 2 * points, 2 * slabs * window)
    txb = txb.reshape(COUNT, 2 * slabs * window, 2 * points)
    tzb = np.stack([np.concatenate([cos, -sin], 1)[z_of], np.concatenate([sin, cos], 1)[z_of]], 1) * fwd
    return tz, ty, tx, txb, tyb, tzb


def fused_kernel(
    sizes,
    coef_hbm, reach, occ, ext_hbm, absk, square, tz, ty_hbm, tx_hbm, txb_hbm, tyb_hbm, tzb_hbm,
    out, pot,
    coef, ext, ty, tx, txb, tyb, tzb, column,
    xh, xl, send, recv, sendb, recvb, wave, dens, weights, vlow, vhigh, vwide,
    load_sem, send_sem, recv_sem, sendb_sem, recvb_sem, v_send, v_recv, w_send, w_recv,
):
    nbands, planes, width, slabs, groups, own = sizes
    points = 2 * width
    doubled = 2 * width
    chunks = own // COUNT
    members = groups * slabs
    rows = COUNT * planes
    block = slabs * rows
    tiles = nbands * doubled // 128
    window = 16
    group = lax.axis_index("band")
    slab = lax.axis_index("slab")
    me = group * slabs + slab

    barrier = pltpu.get_barrier_semaphore()

    def greet(step, carry):
        other = lax.rem(me + step, members)
        pl.semaphore_signal(barrier, inc=1, device_id=(other // slabs, lax.rem(other, slabs)), device_id_type=MESH)
        return carry

    lax.fori_loop(1, members, greet, 0)

    def at_block(ref, chunk, member):
        return ref.at[chunk, pl.ds(pl.multiple_of(member * tiles * rows, 8), tiles * rows), :]

    loads = [
        pltpu.make_async_copy(source, target, load_sem.at[place])
        for place, (source, target) in enumerate([
            (coef_hbm, coef), (ty_hbm, ty), (tx_hbm, tx), (ext_hbm, ext), (txb_hbm, txb), (tyb_hbm, tyb), (tzb_hbm, tzb)
        ])
    ]
    for load in loads:
        load.start()

    turned_reach = reach[...].astype(jnp.float32).T
    for gx in range(planes):
        column[gx] = jnp.broadcast_to(turned_reach[:, gx:gx + 1], (width, 128))

    def keep_of(gx):
        return absk[...] <= column[gx][:, 0:1]

    loads[0].wait()

    def prepare(gx, carry):
        pieces = []
        keep = keep_of(gx)
        for b in range(nbands):
            value = jnp.where(keep, coef[b, gx], 0.0)
            pieces.append(value)
            pieces.append(jnp.concatenate([value[:, width:], -value[:, :width]], axis=1))
        high, low = split(jnp.concatenate(pieces, axis=0))
        xh[gx] = high
        xl[gx] = low
        return carry

    lax.fori_loop(0, planes, prepare, 0)

    def z_spread(chunk):
        def one(gx, carry):
            high, low = xh[gx], xl[gx]
            value = dot_t(tz[0, chunk], high) + dot_t(tz[1, chunk], high) + dot_t(tz[0, chunk], low)
            for p in range(COUNT):
                for tile in range(tiles):
                    start = tile * rows + p * planes + gx
                    piece = value[p * members:(p + 1) * members, tile * 128:(tile + 1) * 128]
                    send[chunk, pl.ds(start, members, stride=tiles * rows), :] = piece
            return carry

        lax.fori_loop(0, planes, one, 0)

    def other_of(step):
        turn = lax.rem(step + slabs // 2, slabs)
        return lax.rem(group + step // slabs, groups), lax.rem(slab + turn, slabs)

    def push(chunk, from_ref, to_ref, sems, rsems, tgroup, tslab):
        pltpu.make_async_remote_copy(
            src_ref=at_block(from_ref, chunk, tgroup * slabs + tslab),
            dst_ref=at_block(to_ref, chunk, me),
            send_sem=sems.at[chunk],
            recv_sem=rsems.at[chunk],
            device_id=(tgroup, tslab),
            device_id_type=MESH,
        ).start()

    def keep_own(chunk, from_ref, to_ref, rsems):
        pltpu.make_async_copy(at_block(from_ref, chunk, me), at_block(to_ref, chunk, me), rsems.at[chunk]).start()

    def spread_out(chunk):
        z_spread(chunk)

        def one(step, carry):
            tgroup, tslab = other_of(step)

            @pl.when(tgroup * slabs + tslab != me)
            def _():
                push(chunk, send, recv, send_sem, recv_sem, tgroup, tslab)

            return carry

        lax.fori_loop(0, members, one, 0)
        keep_own(chunk, send, recv, recv_sem)

    def wait_all(ref, sems, chunk):
        pltpu.make_async_copy(ref.at[chunk], ref.at[chunk], sems.at[chunk]).wait()

    def share_planes(step, ref_at, send_at, recv_at):
        tgroup = lax.rem(group + step, groups)
        pltpu.make_async_remote_copy(
            src_ref=ref_at, dst_ref=ref_at, send_sem=send_at, recv_sem=recv_at,
            device_id=(tgroup, slab), device_id_type=MESH,
        ).start()

    pl.semaphore_wait(barrier, members - 1)

    for b in range(nbands):
        weights[group, b] = jnp.full((8, 128), occ[b].astype(jnp.float32) * (1.0 / (nbands * groups)))
    for step in range(1, groups):
        share_planes(step, weights.at[group], w_send.at[0], w_recv.at[0])

    for chunk in range(chunks):
        spread_out(chunk)

    others = weights.at[pl.ds(0, groups - 1)]
    pltpu.make_async_copy(others, others, w_recv.at[0]).wait()
    pltpu.make_async_copy(others, others, w_send.at[0]).wait()

    for load in loads[1:]:
        load.wait()

    def middle(chunk, carry):
        wait_all(recv, recv_sem, chunk)
        dens[...] = jnp.zeros_like(dens)

        def build(g, carry):
            arrived = recv[chunk, pl.ds(pl.multiple_of(g * tiles * block, 8), tiles * block), :]
            arrived = arrived.reshape(slabs, tiles, rows, 128)
            high, low = split(
                jnp.concatenate([arrived[:, tile].reshape(block, 128) for tile in range(tiles)], axis=1)
            )
            for b in range(nbands):
                first = b * 128
                lh = high[:, first:first + doubled + 64]
                ll = low[:, first:first + doubled + 64]
                parts = []
                for c in range(2):
                    y = dot(lh, ty[0, b, c]) + dot(lh, ty[1, b, c]) + dot(ll, ty[0, b, c])
                    parts.append(y.reshape(slabs, rows, points))
                w = weights[g, b, 0:1, 0:1]
                for p in range(COUNT):
                    lead = p * (rows - window)
                    stacked = jnp.concatenate(
                        [part[:, lead:lead + window].reshape(slabs * window, points) for part in parts], axis=0
                    )
                    yh, yl = split(stacked)
                    field = dot(tx[0, p], yh) + dot(tx[1, p], yh) + dot(tx[0, p], yl)
                    wave[p, g * nbands + b] = field
                    dens[p] += w * (field[:points] * field[:points] + field[points:] * field[points:])
            return carry

        lax.fori_loop(0, groups, build, 0)
        potentials = []
        for p in range(COUNT):
            d = dens[p]
            outer = ext[:, pl.ds(group * own + chunk * COUNT + p, 1), :].reshape(points, points)
            potential = outer - SLATER * jnp.exp(jnp.log(d) * (1.0 / 3.0))
            potentials.append(potential)
            dens[p] = potential
        place = group * chunks + chunk
        low_rows = pl.ds(pl.multiple_of(place * COUNT * points, 8), COUNT * points)
        high_rows = pl.ds(pl.multiple_of(place * points, 8), points)
        vlow[low_rows, :] = jnp.concatenate([value[:, :128] for value in potentials], axis=0)
        vhigh[high_rows, :] = jnp.concatenate([value[:, 128:] for value in potentials], axis=1)
        for step in range(1, groups):
            share_planes(step, vlow.at[low_rows], v_send.at[0], v_recv.at[0])
            share_planes(step, vhigh.at[high_rows], v_send.at[1], v_recv.at[1])

        def back(turn, carry):
            g = lax.rem(group + turn, groups)
            sums = []
            for b in range(nbands):
                boths = []
                for p in range(COUNT):
                    potential = dens[p]
                    field = wave[p, g * nbands + b]
                    product = jnp.concatenate([field[:points] * potential, field[points:] * potential], axis=0)
                    ph, pll = split(product)
                    boths.append(dot(txb[0, p], ph) + dot(txb[1, p], ph) + dot(txb[0, p], pll))
                total = None
                for c in range(2):
                    low_rows, high_rows = [
                        both[c * slabs * window:(c + 1) * slabs * window].reshape(slabs, window, points) for both in boths
                    ]
                    cut = rows - window
                    merged = jnp.concatenate(
                        [low_rows[:, :cut], low_rows[:, cut:] + high_rows[:, :window - cut], high_rows[:, window - cut:]], axis=1
                    ).reshape(block, points)
                    mh, ml = split(merged)
                    value = dot(mh, tyb[0, b, c]) + dot(mh, tyb[1, b, c]) + dot(ml, tyb[0, b, c])
                    total = value if total is None else total + value
                sums.append(total)
            first, second = sums
            pieces = [first[:, :128], first[:, 128:] + second[:, :128], second[:, 128:]]
            sendb[chunk, pl.ds(pl.multiple_of(g * tiles * block, 8), tiles * block), :] = jnp.concatenate(
                [piece.reshape(slabs, 1, rows, 128) for piece in pieces], axis=1
            ).reshape(tiles * block, 128)

            def one(step, carry):
                tslab = lax.rem(slab + step + slabs // 2, slabs)

                @pl.when(g * slabs + tslab != me)
                def _():
                    push(chunk, sendb, recvb, sendb_sem, recvb_sem, g, tslab)

                return carry

            lax.fori_loop(0, slabs, one, 0)
            return carry

        lax.fori_loop(0, groups, back, 0)
        keep_own(chunk, sendb, recvb, recvb_sem)
        return carry

    lax.fori_loop(0, chunks, middle, 0)

    def z_back(chunk):
        wait_all(recvb, recvb_sem, chunk)

        def one(gx, carry):
            columns = []
            for tile in range(tiles):
                starts = [tile * rows + p * planes + gx for p in range(COUNT)]
                columns.append(jnp.concatenate(
                    [recvb[chunk, pl.ds(start, members, stride=tiles * rows), :] for start in starts], axis=0
                ))
            turned = jnp.concatenate(columns, axis=1).T
            high, low = split(turned)
            for b in range(nbands):
                total = None
                for c in range(2):
                    first = (b * 2 + c) * width
                    th, tl = high[first:first + width], low[first:first + width]
                    part = dot(th, tzb[0, chunk, c]) + dot(th, tzb[1, chunk, c]) + dot(tl, tzb[0, chunk, c])
                    total = part if total is None else total + part
                if chunk > 0:
                    total = total + out[b, gx]
                if chunk == chunks - 1:
                    index = slab * planes + gx
                    freq = jnp.where(index < width // 2, index, index - width)
                    kinetic = KINETIC * ((freq * freq).astype(jnp.float32) + square[...])
                    total = jnp.where(keep_of(gx), kinetic * coef[b, gx] + total, 0.0)
                out[b, gx] = total
            return carry

        lax.fori_loop(0, planes, one, 0)

    def wait_planes(sems):
        for place, ref in enumerate((vlow, vhigh)):
            given = ref.at[pl.ds(0, (groups - 1) * (ref.shape[0] // groups))]
            pltpu.make_async_copy(given, given, sems.at[place]).wait()

    for chunk in range(chunks - 1):
        z_back(chunk)

    wait_planes(v_recv)
    half = points - 128

    def widen(place, carry):
        value = vhigh[pl.ds(pl.multiple_of(place * points, 8), points), :]
        vwide[pl.ds(pl.multiple_of(place * COUNT * points, 8), points), :] = value
        vwide[pl.ds(pl.multiple_of((place * COUNT + 1) * points, 8), points), :] = pltpu.roll(value, half, 1)
        return carry

    lax.fori_loop(0, groups * chunks, widen, 0)
    layers = own * groups

    def place_row(x, carry):
        first = vlow[pl.ds(x, layers, stride=points), :]
        second = vwide[pl.ds(x, layers, stride=points), :]
        pot[x] = jnp.concatenate([first, second[:, :half]], axis=1)
        return carry

    lax.fori_loop(0, points, place_row, 0)
    z_back(chunks - 1)

    def wait_sent(ref, sems, chunk):
        sent = ref.at[chunk, pl.ds(0, (members - 1) * tiles * rows), :]
        pltpu.make_async_copy(sent, sent, sems.at[chunk]).wait()

    for chunk in range(chunks):
        wait_sent(send, send_sem, chunk)
        wait_sent(sendb, sendb_sem, chunk)
    wait_planes(v_send)


def fused_plan(coefficients, occupation, pencil_reach, external):
    nbands, planes, width, doubled = coefficients.shape
    points = 2 * width
    slabs = lax.axis_size("slab")
    groups = lax.axis_size("band")
    layers = points // slabs
    own = layers // groups
    chunks = own // COUNT
    members = groups * slabs
    rows = COUNT * planes
    lanes = nbands * doubled
    tables = [
        jnp.asarray(np.stack(split_np(table)))
        for table in fused_tables(width, nbands, planes, slabs, groups, own)
    ]
    wavenumbers = np.where(np.arange(width) < width // 2, np.arange(width), np.arange(width) - width)
    twice = np.concatenate([wavenumbers, wavenumbers])
    absk = jnp.asarray(np.abs(twice)[None].astype(np.float32))
    square = jnp.asarray((wavenumbers[:, None] ** 2 + twice[None] ** 2).astype(np.float32))
    vmem = pl.BlockSpec(memory_space=pltpu.VMEM)
    smem = pl.BlockSpec(memory_space=pltpu.SMEM)
    hbm = pl.BlockSpec(memory_space=pl.ANY)
    operands = [coefficients, pencil_reach, occupation, external, absk, square] + tables
    bf, f32 = jnp.bfloat16, jnp.float32
    dma = pltpu.SemaphoreType.DMA
    exchange = pltpu.VMEM((chunks, members * rows * lanes // 128, 128), f32)
    mixed = pltpu.VMEM((planes, nbands * 2 * width, doubled), bf)
    return pl.pallas_call(
        functools.partial(fused_kernel, (nbands, planes, width, slabs, groups, own)),
        name="fused",
        out_shape=[
            jax.ShapeDtypeStruct(coefficients.shape, f32),
            jax.ShapeDtypeStruct(external.shape, f32),
        ],
        in_specs=[hbm, vmem, smem, hbm, vmem, vmem, vmem] + [hbm] * 5,
        out_specs=[vmem, vmem],
        scratch_shapes=[
            pltpu.VMEM(coefficients.shape, f32),
            pltpu.VMEM(external.shape, f32),
        ] + [pltpu.VMEM(table.shape, bf) for table in tables[1:]] + [
            pltpu.VMEM((planes, width, 128), f32),
            mixed, mixed, exchange, exchange, exchange, exchange,
            pltpu.VMEM((COUNT, groups * nbands, 2 * points, points), f32),
            pltpu.VMEM((COUNT, points, points), f32),
            pltpu.VMEM((groups, nbands, 8, 128), f32),
            pltpu.VMEM((layers * points, 128), f32),
            pltpu.VMEM((groups * chunks * points, 128), f32),
            pltpu.VMEM((layers * points, 128), f32),
            dma((7,)), dma((chunks,)), dma((chunks,)), dma((chunks,)), dma((chunks,)),
            dma((2,)), dma((2,)), dma((1,)), dma((1,)),
        ],
        compiler_params=pltpu.CompilerParams(
            collective_id=0, has_side_effects=True, vmem_limit_bytes=58 * 2**20
        ),
    )(*operands)


def shards(coefficients, occupation, pencil_reach, external):
    nbands, planes, width, doubled = coefficients.shape
    slabs, groups = lax.axis_size("slab"), lax.axis_size("band")
    layers = doubled // slabs
    fits = (
        layers % (groups * COUNT) == 0 and nbands == 2 and planes == 12 and width == 96 and COUNT == 2
    )
    plan = fused_plan if fits else slab_plan
    return plan(coefficients, occupation, pencil_reach, external)


def solution(mesh):
    return jax.shard_map(
        shards,
        mesh=mesh,
        in_specs=(P("band", "slab", None, None), P("band"), P("slab", None), P(None, "slab", None)),
        out_specs=(P("band", "slab", None, None), P(None, "slab", None)),
        check_vma=False,
    )
```

```python
import functools
import math

import jax
import jax.numpy as jnp
import ml_dtypes
import numpy as np
from jax import lax
from jax.experimental import pallas as pl
from jax.experimental.pallas import tpu as pltpu
from jax.sharding import PartitionSpec as P

KINETIC = 0.0005
SLATER = 0.9847
COUNT = 2
UNROLL = 3
MESH = pl.DeviceIdType.MESH


def frequency(length):
    indices = jnp.arange(length, dtype=jnp.int32)
    return jnp.where(indices < length // 2, indices, indices - length)


def inverse_table(length, extent):
    wavenumbers = frequency(length)
    positions = jnp.arange(extent, dtype=jnp.int32)
    phases = positions[:, None] * wavenumbers[None, :] % extent
    angles = phases.astype(jnp.float32) * (2.0 * math.pi / extent)
    factor = length ** (-0.5)
    cosine = jnp.cos(angles) * factor
    sine_part = jnp.sin(angles) * factor
    return jnp.stack([jnp.stack([cosine, -sine_part], 1), jnp.stack([sine_part, cosine], 1)], 0)


def forward_table(length, extent):
    wavenumbers = frequency(length)
    positions = jnp.arange(extent, dtype=jnp.int32)
    phases = wavenumbers[:, None] * positions[None, :] % extent
    angles = phases.astype(jnp.float32) * (2.0 * math.pi / extent)
    factor = length**0.5 / extent
    cosine = jnp.cos(angles) * factor
    sine_part = jnp.sin(angles) * factor
    return jnp.stack([jnp.stack([cosine, sine_part], 1), jnp.stack([-sine_part, cosine], 1)], 0)


def contract(form, left, right):
    return jnp.einsum(form, left, right, precision=lax.Precision.HIGH)


def slab_plan(coefficients, occupation, pencil_reach, external):
    nbands, planes, width, doubled = coefficients.shape
    points = 2 * width
    slabs = lax.axis_size("slab")
    layers = points // slabs
    groups = lax.axis_size("band")
    inverse = inverse_table(width, points)
    forward = forward_table(width, points)
    wavenumbers = frequency(width)
    sphere = (jnp.abs(wavenumbers)[None, None, :] <= pencil_reach[:, :, None]).astype(jnp.float32)
    sphere_full = sphere[None, :, :, None, :]
    masked = coefficients.reshape(nbands, planes, width, 2, width) * sphere_full
    along_z = contract("bxgci,onci->bxnog", masked, inverse)
    flattened = along_z.reshape(nbands, planes, points, 2 * width)
    received = lax.all_to_all(flattened, "slab", split_axis=2, concat_axis=1, tiled=True)
    columns = received.reshape(received.shape[0], width, layers, 2, width)
    spread = contract("bkzcg,oycg->bkzoy", columns, inverse)
    wavefield = contract("bkzcy,oxck->bxzoy", spread, inverse)
    squares = jnp.sum(wavefield * wavefield, axis=3)
    weights = occupation.astype(jnp.float32) / (nbands * groups)
    partial_value = contract("b,bxzy->xzy", weights, squares)
    rows_all = points * layers
    share = (rows_all + groups - 1) // groups
    flat_partial = partial_value.reshape(rows_all, points)
    density = lax.psum_scatter(flat_partial, "band", scatter_dimension=0, tiled=True)
    flat_external = external.reshape(rows_all, points)
    start_row = lax.axis_index("band") * share
    own_external = lax.dynamic_slice_in_dim(flat_external, start_row, share, 0)
    own_potential = own_external - SLATER * jnp.cbrt(density)
    gathered = lax.all_gather(own_potential, "band", axis=0, tiled=True)
    potential_all = gathered.reshape(points, layers, points)
    product = wavefield * potential_all[None, :, :, None, :]
    back_rows = contract("bxzcy,okcx->bkzoy", product, forward)
    back_y = contract("bkzcy,ogcy->bkzog", back_rows, forward).reshape(
        nbands, width, layers, 2 * width
    )
    received = lax.all_to_all(back_y, "slab", split_axis=1, concat_axis=2, tiled=True)
    blocks = received.reshape(received.shape[0], planes, points, 2, width)
    returned = contract("bxncg,ohcn->bxgoh", blocks, forward)
    plane_index = lax.axis_index("slab") * planes + jnp.arange(planes, dtype=jnp.int32)
    plane_freq = jnp.where(plane_index < width // 2, plane_index, plane_index - width)
    plane_sq = (plane_freq * plane_freq).astype(jnp.float32)
    wave_sq = (wavenumbers * wavenumbers).astype(jnp.float32)
    kinetic = KINETIC * (plane_sq[:, None, None] + wave_sq[None, :, None] + wave_sq[None, None, :])
    finished = sphere_full * (kinetic[None, :, :, None, :] * masked + returned)
    return (finished.reshape(nbands, planes, width, 2 * width), potential_all)


def split_np(table):
    high = table.astype(ml_dtypes.bfloat16)
    low = (table - high.astype(np.float64)).astype(ml_dtypes.bfloat16)
    return high, low


def split(value):
    high = value.astype(jnp.bfloat16)
    low = (value - high.astype(jnp.float32)).astype(jnp.bfloat16)
    return high, low


def dot(left, right):
    return jnp.dot(left, right, preferred_element_type=jnp.float32)


def dot_t(left, right):
    return lax.dot_general(left, right, (((1,), (1,)), ((), ())), preferred_element_type=jnp.float32)


def fused_tables(width, nbands, planes, slabs, groups, own):
    points = 2 * width
    doubled = 2 * width
    layers = points // slabs
    chunks = own // COUNT
    rows = COUNT * planes
    indices = np.arange(width)
    wave = np.where(indices < width // 2, indices, indices - width)
    phase = (np.arange(points)[:, None] * wave[None, :]) % points
    angles = phase * (2.0 * math.pi / points)
    cos, sin = np.cos(angles), np.sin(angles)
    inv = width**-0.5
    fwd = width**0.5 / points
    z_of = np.array(
        [
            [
                s * layers + g * own + part * COUNT + p
                for p in range(COUNT)
                for g in range(groups)
                for s in range(slabs)
            ]
            for part in range(chunks)
        ]
    )
    tz = np.concatenate([cos, -sin], 1)[z_of] * inv
    span = doubled + 64
    ty = np.zeros((nbands, 2, span, points))
    tyb = np.zeros((nbands, 2, points, span))
    for b in range(nbands):
        shift = b * doubled - b * 128
        ty[b, 0, shift:shift + width] = cos.T * inv
        ty[b, 0, shift + width:shift + doubled] = -sin.T * inv
        ty[b, 1, shift:shift + width] = sin.T * inv
        ty[b, 1, shift + width:shift + doubled] = cos.T * inv
        tyb[b, 0, :, shift:shift + width] = cos * fwd
        tyb[b, 0, :, shift + width:shift + doubled] = -sin * fwd
        tyb[b, 1, :, shift:shift + width] = sin * fwd
        tyb[b, 1, :, shift + width:shift + doubled] = cos * fwd
    window = 16
    tx = np.zeros((COUNT, 2, points, 2, slabs, window))
    txb = np.zeros((COUNT, 2, slabs, window, 2, points))
    for p in range(COUNT):
        first = p * planes - p * (rows - window)
        put = slice(first, first + planes)
        c3 = cos.reshape(points, slabs, planes)
        s3 = sin.reshape(points, slabs, planes)
        tx[p, 0, :, 0][:, :, put] = c3 * inv
        tx[p, 0, :, 1][:, :, put] = -s3 * inv
        tx[p, 1, :, 0][:, :, put] = s3 * inv
        tx[p, 1, :, 1][:, :, put] = c3 * inv
        ct, st = c3.transpose(1, 2, 0), s3.transpose(1, 2, 0)
        txb[p, 0][:, put, 0] = ct * fwd
        txb[p, 0][:, put, 1] = st * fwd
        txb[p, 1][:, put, 0] = -st * fwd
        txb[p, 1][:, put, 1] = ct * fwd
    tx = tx.reshape(COUNT, 2 * points, 2 * slabs * window)
    txb = txb.reshape(COUNT, 2 * slabs * window, 2 * points)
    tzb = np.stack([np.concatenate([cos, -sin], 1)[z_of], np.concatenate([sin, cos], 1)[z_of]], 1) * fwd
    return tz, ty, tx, txb, tyb, tzb


def fused_kernel(
    sizes,
    coef_hbm, reach_hbm, occ, ext_hbm, square_hbm, tz_hbm, ty_hbm, tx_hbm, txb_hbm, tyb_hbm, tzb_hbm,
    out, pot,
    coef, reach, ext, square, tz, ty, tx, txb, tyb, tzb, column,
    xh, xl, send, recv, sendb, recvb, wave, dens, weights, vlow, vhigh, vwide,
    load_sem, send_sem, recv_sem, sendb_sem, recvb_sem, v_send, v_recv, w_send, w_recv,
):
    nbands, planes, width, slabs, groups, own = sizes
    points = 2 * width
    doubled = 2 * width
    chunks = own // COUNT
    members = groups * slabs
    rows = COUNT * planes
    block = slabs * rows
    tiles = nbands * doubled // 128
    window = 16
    group = lax.axis_index("band")
    slab = lax.axis_index("slab")
    me = group * slabs + slab

    def at_block(ref, chunk, member):
        return ref.at[chunk, pl.ds(pl.multiple_of(member * tiles * rows, 8), tiles * rows), :]

    loads = [
        pltpu.make_async_copy(source, target, load_sem.at[place])
        for place, (source, target) in enumerate([
            (reach_hbm, reach), (tz_hbm, tz), (coef_hbm, coef),
            (ty_hbm, ty), (tx_hbm, tx), (ext_hbm, ext), (txb_hbm, txb), (tyb_hbm, tyb), (tzb_hbm, tzb),
            (square_hbm, square),
        ])
    ]
    for load in loads:
        load.start()

    barrier = pltpu.get_barrier_semaphore()

    def greet(step, carry):
        other = lax.rem(me + step, members)
        pl.semaphore_signal(barrier, inc=1, device_id=(other // slabs, lax.rem(other, slabs)), device_id_type=MESH)
        return carry

    lax.fori_loop(1, members, greet, 0)

    lane = lax.rem(lax.broadcasted_iota(jnp.int32, (1, doubled), 1), width)
    absk = jnp.where(lane < width // 2, lane, width - lane).astype(jnp.float32)

    loads[0].wait()
    turned_reach = reach[...].astype(jnp.float32).T
    for gx in range(planes):
        column[gx] = jnp.broadcast_to(turned_reach[:, gx:gx + 1], (width, 128))

    def keep_of(gx):
        return absk <= column[gx][:, 0:1]

    def prepare(gx):
        pieces = []
        keep = keep_of(gx)
        for b in range(nbands):
            value = jnp.where(keep, coef[b, gx], 0.0)
            pieces.append(value)
            pieces.append(jnp.concatenate([value[:, width:], -value[:, :width]], axis=1))
        high, low = split(jnp.concatenate(pieces, axis=0))
        xh[gx] = high
        xl[gx] = low

    def z_spread(chunk):
        zs = COUNT * members

        def some(turn, carry):
            for gx in [turn * UNROLL + place for place in range(UNROLL)]:
                if chunk == 0:
                    prepare(gx)
                both = dot_t(tz[chunk], xh[gx])
                value = both[:zs] + both[zs:] + dot_t(tz[chunk, :zs], xl[gx])
                for p in range(COUNT):
                    for tile in range(tiles):
                        start = tile * rows + p * planes + gx
                        piece = value[p * members:(p + 1) * members, tile * 128:(tile + 1) * 128]
                        send[chunk, pl.ds(start, members, stride=tiles * rows), :] = piece
            return carry

        lax.fori_loop(0, planes // UNROLL, some, 0)

    half = slabs // 2

    def slab_at(turn):
        side = lax.rem(slab // half + 1 + turn // half, 2)
        return side * half + lax.rem(slab + turn, half)

    def other_of(step):
        return lax.rem(group + lax.rem(step, groups), groups), slab_at(step // groups)

    def push(chunk, from_ref, to_ref, sems, rsems, tgroup, tslab):
        pltpu.make_async_remote_copy(
            src_ref=at_block(from_ref, chunk, tgroup * slabs + tslab),
            dst_ref=at_block(to_ref, chunk, me),
            send_sem=sems.at[chunk],
            recv_sem=rsems.at[chunk],
            device_id=(tgroup, tslab),
            device_id_type=MESH,
        ).start()

    def keep_own(chunk, from_ref, to_ref, rsems):
        pltpu.make_async_copy(at_block(from_ref, chunk, me), at_block(to_ref, chunk, me), rsems.at[chunk]).start()

    def spread_out(chunk):
        def one(step, carry):
            tgroup, tslab = other_of(step)

            @pl.when(tgroup * slabs + tslab != me)
            def _():
                push(chunk, send, recv, send_sem, recv_sem, tgroup, tslab)

            return carry

        lax.fori_loop(0, members, one, 0)
        keep_own(chunk, send, recv, recv_sem)

    def wait_all(ref, sems, chunk):
        pltpu.make_async_copy(ref.at[chunk], ref.at[chunk], sems.at[chunk]).wait()

    def share_planes(step, ref_at, send_at, recv_at):
        tgroup = lax.rem(group + step, groups)
        pltpu.make_async_remote_copy(
            src_ref=ref_at, dst_ref=ref_at, send_sem=send_at, recv_sem=recv_at,
            device_id=(tgroup, slab), device_id_type=MESH,
        ).start()

    for b in range(nbands):
        weights[group, b] = jnp.full((8, 128), occ[b].astype(jnp.float32) * (1.0 / (nbands * groups)))
    loads[1].wait()
    loads[2].wait()
    z_spread(0)
    pl.semaphore_wait(barrier, members - 1)
    spread_out(0)
    for step in range(1, groups):
        share_planes(step, weights.at[group], w_send.at[0], w_recv.at[0])

    for chunk in range(1, chunks):
        z_spread(chunk)
        spread_out(chunk)

    others = weights.at[pl.ds(0, groups - 1)]
    pltpu.make_async_copy(others, others, w_recv.at[0]).wait()
    pltpu.make_async_copy(others, others, w_send.at[0]).wait()

    for load in loads[3:]:
        load.wait()

    def middle(chunk, carry):
        wait_all(recv, recv_sem, chunk)
        dens[...] = jnp.zeros_like(dens)

        def build(g, carry):
            arrived = recv[chunk, pl.ds(pl.multiple_of(g * tiles * block, 8), tiles * block), :]
            arrived = arrived.reshape(slabs, tiles, rows, 128)
            high, low = split(
                jnp.concatenate([arrived[:, tile].reshape(block, 128) for tile in range(tiles)], axis=1)
            )
            for b in range(nbands):
                first = b * 128
                lh = high[:, first:first + doubled + 64]
                ll = low[:, first:first + doubled + 64]
                parts = []
                for c in range(2):
                    y = dot(lh, ty[0, b, c]) + dot(lh, ty[1, b, c]) + dot(ll, ty[0, b, c])
                    parts.append(y.reshape(slabs, rows, points))
                w = weights[g, b, 0:1, 0:1]
                for p in range(COUNT):
                    lead = p * (rows - window)
                    stacked = jnp.concatenate(
                        [part[:, lead:lead + window].reshape(slabs * window, points) for part in parts], axis=0
                    )
                    yh, yl = split(stacked)
                    field = dot(tx[0, p], yh) + dot(tx[1, p], yh) + dot(tx[0, p], yl)
                    wave[p, g * nbands + b] = field
                    dens[p] += w * (field[:points] * field[:points] + field[points:] * field[points:])
            return carry

        lax.fori_loop(0, groups, build, 0)
        potentials = []
        for p in range(COUNT):
            d = dens[p]
            outer = ext[:, pl.ds(group * own + chunk * COUNT + p, 1), :].reshape(points, points)
            potential = outer - SLATER * jnp.exp(jnp.log(d) * (1.0 / 3.0))
            potentials.append(potential)
            dens[p] = potential
        place = group * chunks + chunk
        low_rows = pl.ds(pl.multiple_of(place * COUNT * points, 8), COUNT * points)
        high_rows = pl.ds(pl.multiple_of(place * points, 8), points)
        vlow[low_rows, :] = jnp.concatenate([value[:, :128] for value in potentials], axis=0)
        vhigh[high_rows, :] = jnp.concatenate([value[:, 128:] for value in potentials], axis=1)
        for step in range(1, groups):
            share_planes(step, vlow.at[low_rows], v_send.at[0], v_recv.at[0])
            share_planes(step, vhigh.at[high_rows], v_send.at[1], v_recv.at[1])

        def back(turn, carry):
            g = lax.rem(group + turn, groups)
            sums = []
            for b in range(nbands):
                boths = []
                for p in range(COUNT):
                    potential = dens[p]
                    field = wave[p, g * nbands + b]
                    product = jnp.concatenate([field[:points] * potential, field[points:] * potential], axis=0)
                    ph, pll = split(product)
                    boths.append(dot(txb[0, p], ph) + dot(txb[1, p], ph) + dot(txb[0, p], pll))
                total = None
                for c in range(2):
                    low_rows, high_rows = [
                        both[c * slabs * window:(c + 1) * slabs * window].reshape(slabs, window, points) for both in boths
                    ]
                    cut = rows - window
                    merged = jnp.concatenate(
                        [low_rows[:, :cut], low_rows[:, cut:] + high_rows[:, :window - cut], high_rows[:, window - cut:]], axis=1
                    ).reshape(block, points)
                    mh, ml = split(merged)
                    value = dot(mh, tyb[0, b, c]) + dot(mh, tyb[1, b, c]) + dot(ml, tyb[0, b, c])
                    total = value if total is None else total + value
                sums.append(total)
            first, second = sums
            pieces = [first[:, :128], first[:, 128:] + second[:, :128], second[:, 128:]]
            sendb[chunk, pl.ds(pl.multiple_of(g * tiles * block, 8), tiles * block), :] = jnp.concatenate(
                [piece.reshape(slabs, 1, rows, 128) for piece in pieces], axis=1
            ).reshape(tiles * block, 128)

            def one(step, carry):
                tslab = slab_at(step)

                @pl.when(g * slabs + tslab != me)
                def _():
                    push(chunk, sendb, recvb, sendb_sem, recvb_sem, g, tslab)

                return carry

            lax.fori_loop(0, slabs, one, 0)
            return carry

        lax.fori_loop(0, groups, back, 0)
        keep_own(chunk, sendb, recvb, recvb_sem)
        return carry

    lax.fori_loop(0, chunks, middle, 0)

    def z_back(chunk):
        wait_all(recvb, recvb_sem, chunk)

        def one(gx):
            columns = []
            for tile in range(tiles):
                starts = [tile * rows + p * planes + gx for p in range(COUNT)]
                columns.append(jnp.concatenate(
                    [recvb[chunk, pl.ds(start, members, stride=tiles * rows), :] for start in starts], axis=0
                ))
            turned = jnp.concatenate(columns, axis=1).T
            high, low = split(turned)
            for b in range(nbands):
                total = None
                for c in range(2):
                    first = (b * 2 + c) * width
                    th, tl = high[first:first + width], low[first:first + width]
                    part = dot(th, tzb[0, chunk, c]) + dot(th, tzb[1, chunk, c]) + dot(tl, tzb[0, chunk, c])
                    total = part if total is None else total + part
                if chunk > 0:
                    total = total + out[b, gx]
                if chunk == chunks - 1:
                    index = slab * planes + gx
                    freq = jnp.where(index < width // 2, index, index - width)
                    kinetic = KINETIC * ((freq * freq).astype(jnp.float32) + square[...])
                    total = jnp.where(keep_of(gx), kinetic * coef[b, gx] + total, 0.0)
                out[b, gx] = total

        def some(turn, carry):
            for place in range(UNROLL):
                one(turn * UNROLL + place)
            return carry

        lax.fori_loop(0, planes // UNROLL, some, 0)

    def wait_planes(sems):
        for place, ref in enumerate((vlow, vhigh)):
            given = ref.at[pl.ds(0, (groups - 1) * (ref.shape[0] // groups))]
            pltpu.make_async_copy(given, given, sems.at[place]).wait()

    for chunk in range(chunks - 1):
        z_back(chunk)

    wait_planes(v_recv)
    spare = points - 128

    def widen(place, carry):
        value = vhigh[pl.ds(pl.multiple_of(place * points, 8), points), :]
        vwide[pl.ds(pl.multiple_of(place * COUNT * points, 8), points), :] = value
        vwide[pl.ds(pl.multiple_of((place * COUNT + 1) * points, 8), points), :] = pltpu.roll(value, spare, 1)
        return carry

    lax.fori_loop(0, groups * chunks, widen, 0)
    layers = own * groups

    def place_row(x, carry):
        first = vlow[pl.ds(x, layers, stride=points), :]
        second = vwide[pl.ds(x, layers, stride=points), :]
        pot[x] = jnp.concatenate([first, second[:, :spare]], axis=1)
        return carry

    lax.fori_loop(0, points, place_row, 0)
    z_back(chunks - 1)

    def wait_sent(ref, sems, chunk):
        sent = ref.at[chunk, pl.ds(0, (members - 1) * tiles * rows), :]
        pltpu.make_async_copy(sent, sent, sems.at[chunk]).wait()

    for chunk in range(chunks):
        wait_sent(send, send_sem, chunk)
        wait_sent(sendb, sendb_sem, chunk)
    wait_planes(v_send)


def fused_plan(coefficients, occupation, pencil_reach, external):
    nbands, planes, width, doubled = coefficients.shape
    points = 2 * width
    slabs = lax.axis_size("slab")
    groups = lax.axis_size("band")
    layers = points // slabs
    own = layers // groups
    chunks = own // COUNT
    members = groups * slabs
    rows = COUNT * planes
    lanes = nbands * doubled
    first, *rest = fused_tables(width, nbands, planes, slabs, groups, own)
    tables = [jnp.asarray(np.concatenate(split_np(first), axis=1))]
    tables += [jnp.asarray(np.stack(split_np(table))) for table in rest]
    wavenumbers = np.where(np.arange(width) < width // 2, np.arange(width), np.arange(width) - width)
    twice = np.concatenate([wavenumbers, wavenumbers])
    square = jnp.asarray((wavenumbers[:, None] ** 2 + twice[None] ** 2).astype(np.float32))
    vmem = pl.BlockSpec(memory_space=pltpu.VMEM)
    smem = pl.BlockSpec(memory_space=pltpu.SMEM)
    hbm = pl.BlockSpec(memory_space=pl.ANY)
    operands = [coefficients, pencil_reach, occupation, external, square] + tables
    bf, f32 = jnp.bfloat16, jnp.float32
    dma = pltpu.SemaphoreType.DMA
    exchange = pltpu.VMEM((chunks, members * rows * lanes // 128, 128), f32)
    mixed = pltpu.VMEM((planes, nbands * 2 * width, doubled), bf)
    return pl.pallas_call(
        functools.partial(fused_kernel, (nbands, planes, width, slabs, groups, own)),
        name="fused",
        out_shape=[
            pltpu.VMEM(coefficients.shape, f32),
            pltpu.VMEM(external.shape, f32),
        ],
        in_specs=[hbm, hbm, smem, hbm, hbm] + [hbm] * len(tables),
        out_specs=[vmem, vmem],
        scratch_shapes=[
            pltpu.VMEM(coefficients.shape, f32),
            pltpu.VMEM(pencil_reach.shape, jnp.int32),
            pltpu.VMEM(external.shape, f32),
            pltpu.VMEM(square.shape, f32),
        ] + [pltpu.VMEM(table.shape, bf) for table in tables] + [
            pltpu.VMEM((planes, width, 128), f32),
            mixed, mixed, exchange, exchange, exchange, exchange,
            pltpu.VMEM((COUNT, groups * nbands, 2 * points, points), f32),
            pltpu.VMEM((COUNT, points, points), f32),
            pltpu.VMEM((groups, nbands, 8, 128), f32),
            pltpu.VMEM((layers * points, 128), f32),
            pltpu.VMEM((groups * chunks * points, 128), f32),
            pltpu.VMEM((layers * points, 128), f32),
            dma((10,)), dma((chunks,)), dma((chunks,)), dma((chunks,)), dma((chunks,)),
            dma((2,)), dma((2,)), dma((1,)), dma((1,)),
        ],
        compiler_params=pltpu.CompilerParams(
            collective_id=0, has_side_effects=True, vmem_limit_bytes=52 * 2**20
        ),
    )(*operands)


def shards(coefficients, occupation, pencil_reach, external):
    nbands, planes, width, doubled = coefficients.shape
    slabs, groups = lax.axis_size("slab"), lax.axis_size("band")
    layers = doubled // slabs
    fits = (
        layers % (groups * COUNT) == 0 and nbands == 2 and planes == 12 and width == 96 and slabs % 2 == 0
    )
    plan = fused_plan if fits else slab_plan
    return plan(coefficients, occupation, pencil_reach, external)


def solution(mesh):
    return jax.shard_map(
        shards,
        mesh=mesh,
        in_specs=(P("band", "slab", None, None), P("band"), P("slab", None), P(None, "slab", None)),
        out_specs=(P("band", "slab", None, None), P(None, "slab", None)),
        check_vma=False,
    )
```

```python
import functools
import math

import jax
import jax.numpy as jnp
import ml_dtypes
import numpy as np
from jax import lax
from jax.experimental import pallas as pl
from jax.experimental.pallas import tpu as pltpu
from jax.sharding import PartitionSpec as P

KINETIC = 0.0005
SLATER = 0.9847
COUNT = 2
UNROLL = 3
MESH = pl.DeviceIdType.MESH


def frequency(length):
    indices = jnp.arange(length, dtype=jnp.int32)
    return jnp.where(indices < length // 2, indices, indices - length)


def inverse_table(length, extent):
    wavenumbers = frequency(length)
    positions = jnp.arange(extent, dtype=jnp.int32)
    phases = positions[:, None] * wavenumbers[None, :] % extent
    angles = phases.astype(jnp.float32) * (2.0 * math.pi / extent)
    factor = length ** (-0.5)
    cosine = jnp.cos(angles) * factor
    sine_part = jnp.sin(angles) * factor
    return jnp.stack([jnp.stack([cosine, -sine_part], 1), jnp.stack([sine_part, cosine], 1)], 0)


def forward_table(length, extent):
    wavenumbers = frequency(length)
    positions = jnp.arange(extent, dtype=jnp.int32)
    phases = wavenumbers[:, None] * positions[None, :] % extent
    angles = phases.astype(jnp.float32) * (2.0 * math.pi / extent)
    factor = length**0.5 / extent
    cosine = jnp.cos(angles) * factor
    sine_part = jnp.sin(angles) * factor
    return jnp.stack([jnp.stack([cosine, sine_part], 1), jnp.stack([-sine_part, cosine], 1)], 0)


def contract(form, left, right):
    return jnp.einsum(form, left, right, precision=lax.Precision.HIGH)


def slab_plan(coefficients, occupation, pencil_reach, external):
    nbands, planes, width, doubled = coefficients.shape
    points = 2 * width
    slabs = lax.axis_size("slab")
    layers = points // slabs
    groups = lax.axis_size("band")
    inverse = inverse_table(width, points)
    forward = forward_table(width, points)
    wavenumbers = frequency(width)
    sphere = (jnp.abs(wavenumbers)[None, None, :] <= pencil_reach[:, :, None]).astype(jnp.float32)
    sphere_full = sphere[None, :, :, None, :]
    masked = coefficients.reshape(nbands, planes, width, 2, width) * sphere_full
    along_z = contract("bxgci,onci->bxnog", masked, inverse)
    flattened = along_z.reshape(nbands, planes, points, 2 * width)
    received = lax.all_to_all(flattened, "slab", split_axis=2, concat_axis=1, tiled=True)
    columns = received.reshape(received.shape[0], width, layers, 2, width)
    spread = contract("bkzcg,oycg->bkzoy", columns, inverse)
    wavefield = contract("bkzcy,oxck->bxzoy", spread, inverse)
    squares = jnp.sum(wavefield * wavefield, axis=3)
    weights = occupation.astype(jnp.float32) / (nbands * groups)
    partial_value = contract("b,bxzy->xzy", weights, squares)
    rows_all = points * layers
    share = (rows_all + groups - 1) // groups
    flat_partial = partial_value.reshape(rows_all, points)
    density = lax.psum_scatter(flat_partial, "band", scatter_dimension=0, tiled=True)
    flat_external = external.reshape(rows_all, points)
    start_row = lax.axis_index("band") * share
    own_external = lax.dynamic_slice_in_dim(flat_external, start_row, share, 0)
    own_potential = own_external - SLATER * jnp.cbrt(density)
    gathered = lax.all_gather(own_potential, "band", axis=0, tiled=True)
    potential_all = gathered.reshape(points, layers, points)
    product = wavefield * potential_all[None, :, :, None, :]
    back_rows = contract("bxzcy,okcx->bkzoy", product, forward)
    back_y = contract("bkzcy,ogcy->bkzog", back_rows, forward).reshape(
        nbands, width, layers, 2 * width
    )
    received = lax.all_to_all(back_y, "slab", split_axis=1, concat_axis=2, tiled=True)
    blocks = received.reshape(received.shape[0], planes, points, 2, width)
    returned = contract("bxncg,ohcn->bxgoh", blocks, forward)
    plane_index = lax.axis_index("slab") * planes + jnp.arange(planes, dtype=jnp.int32)
    plane_freq = jnp.where(plane_index < width // 2, plane_index, plane_index - width)
    plane_sq = (plane_freq * plane_freq).astype(jnp.float32)
    wave_sq = (wavenumbers * wavenumbers).astype(jnp.float32)
    kinetic = KINETIC * (plane_sq[:, None, None] + wave_sq[None, :, None] + wave_sq[None, None, :])
    finished = sphere_full * (kinetic[None, :, :, None, :] * masked + returned)
    return (finished.reshape(nbands, planes, width, 2 * width), potential_all)


def split_np(table):
    high = table.astype(ml_dtypes.bfloat16)
    low = (table - high.astype(np.float64)).astype(ml_dtypes.bfloat16)
    return high, low


def split(value):
    high = value.astype(jnp.bfloat16)
    low = (value - high.astype(jnp.float32)).astype(jnp.bfloat16)
    return high, low


def dot(left, right):
    return jnp.dot(left, right, preferred_element_type=jnp.float32)


def dot_t(left, right):
    return lax.dot_general(left, right, (((1,), (1,)), ((), ())), preferred_element_type=jnp.float32)


def fused_tables(width, nbands, planes, slabs, groups, own):
    points = 2 * width
    doubled = 2 * width
    layers = points // slabs
    chunks = own // COUNT
    rows = COUNT * planes
    indices = np.arange(width)
    wave = np.where(indices < width // 2, indices, indices - width)
    phase = (np.arange(points)[:, None] * wave[None, :]) % points
    angles = phase * (2.0 * math.pi / points)
    cos, sin = np.cos(angles), np.sin(angles)
    inv = width**-0.5
    fwd = width**0.5 / points
    z_of = np.array(
        [
            [
                s * layers + g * own + part * COUNT + p
                for p in range(COUNT)
                for g in range(groups)
                for s in range(slabs)
            ]
            for part in range(chunks)
        ]
    )
    tz = np.concatenate([cos, -sin], 1)[z_of] * inv
    span = doubled + 64
    ty = np.zeros((nbands, 2, span, points))
    tyb = np.zeros((nbands, 2, points, span))
    for b in range(nbands):
        shift = b * doubled - b * 128
        ty[b, 0, shift:shift + width] = cos.T * inv
        ty[b, 0, shift + width:shift + doubled] = -sin.T * inv
        ty[b, 1, shift:shift + width] = sin.T * inv
        ty[b, 1, shift + width:shift + doubled] = cos.T * inv
        tyb[b, 0, :, shift:shift + width] = cos * fwd
        tyb[b, 0, :, shift + width:shift + doubled] = -sin * fwd
        tyb[b, 1, :, shift:shift + width] = sin * fwd
        tyb[b, 1, :, shift + width:shift + doubled] = cos * fwd
    window = 16
    tx = np.zeros((COUNT, 2, points, 2, slabs, window))
    txb = np.zeros((COUNT, 2, slabs, window, 2, points))
    for p in range(COUNT):
        first = p * planes - p * (rows - window)
        put = slice(first, first + planes)
        c3 = cos.reshape(points, slabs, planes)
        s3 = sin.reshape(points, slabs, planes)
        tx[p, 0, :, 0][:, :, put] = c3 * inv
        tx[p, 0, :, 1][:, :, put] = -s3 * inv
        tx[p, 1, :, 0][:, :, put] = s3 * inv
        tx[p, 1, :, 1][:, :, put] = c3 * inv
        ct, st = c3.transpose(1, 2, 0), s3.transpose(1, 2, 0)
        txb[p, 0][:, put, 0] = ct * fwd
        txb[p, 0][:, put, 1] = st * fwd
        txb[p, 1][:, put, 0] = -st * fwd
        txb[p, 1][:, put, 1] = ct * fwd
    tx = tx.reshape(COUNT, 2 * points, 2 * slabs * window)
    txb = txb.reshape(COUNT, 2 * slabs * window, 2 * points)
    tzb = np.stack([np.concatenate([cos, -sin], 1)[z_of], np.concatenate([sin, cos], 1)[z_of]], 1) * fwd
    return tz, ty, tx, txb, tyb, tzb


def fused_kernel(
    sizes,
    coef_hbm, reach_hbm, occ, ext_hbm, square_hbm, tz_hbm, ty_hbm, tx_hbm, txb_hbm, tyb_hbm, tzb_hbm,
    out, pot,
    coef, reach, ext, square, tz, ty, tx, txb, tyb, tzb, column,
    xh, xl, send, recv, sendb, recvb, wave, dens, weights, vlow, vhigh, vwide,
    load_sem, send_sem, recv_sem, sendb_sem, recvb_sem, v_send, v_recv, w_send, w_recv,
):
    nbands, planes, width, slabs, groups, own = sizes
    points = 2 * width
    doubled = 2 * width
    chunks = own // COUNT
    members = groups * slabs
    rows = COUNT * planes
    block = slabs * rows
    tiles = nbands * doubled // 128
    window = 16
    zs = COUNT * members
    group = lax.axis_index("band")
    slab = lax.axis_index("slab")
    me = group * slabs + slab

    def at_block(ref, chunk, member):
        return ref.at[chunk, pl.ds(pl.multiple_of(member * tiles * rows, 8), tiles * rows), :]

    loads = [
        pltpu.make_async_copy(source, target, load_sem.at[place])
        for place, (source, target) in enumerate([
            (reach_hbm, reach), (tz_hbm, tz), (coef_hbm, coef),
            (ty_hbm, ty), (tx_hbm, tx), (ext_hbm, ext), (txb_hbm, txb), (tyb_hbm, tyb), (tzb_hbm, tzb),
            (square_hbm, square),
        ])
    ]
    for load in loads:
        load.start()

    barrier = pltpu.get_barrier_semaphore()

    def greet(step, carry):
        other = lax.rem(me + step, members)
        pl.semaphore_signal(barrier, inc=1, device_id=(other // slabs, lax.rem(other, slabs)), device_id_type=MESH)
        return carry

    lax.fori_loop(1, members, greet, 0)

    lane = lax.rem(lax.broadcasted_iota(jnp.int32, (1, doubled), 1), width)
    absk = jnp.where(lane < width // 2, lane, width - lane).astype(jnp.float32)

    loads[0].wait()
    turned_reach = reach[...].astype(jnp.float32).T
    for gx in range(planes):
        column[gx] = jnp.broadcast_to(turned_reach[:, gx:gx + 1], (width, 128))

    def keep_of(gx):
        return absk <= column[gx][:, 0:1]

    def prepare(gx, b):
        value = jnp.where(keep_of(gx), coef[b, gx], 0.0)
        turned = jnp.concatenate([value[:, width:], -value[:, :width]], axis=1)
        high, low = split(jnp.concatenate([value, turned], axis=0))
        xh[gx, b * doubled:(b + 1) * doubled] = high
        xl[gx, b * doubled:(b + 1) * doubled] = low

    def z_planes(chunk, gx, first_tile, last_tile):
        lanes = slice(first_tile * 128, last_tile * 128)
        both = dot_t(tz[chunk], xh[gx, lanes])
        value = both[:zs] + both[zs:] + dot_t(tz[chunk, :zs], xl[gx, lanes])
        for p in range(COUNT):
            for tile in range(first_tile, last_tile):
                start = tile * rows + p * planes + gx
                place = tile - first_tile
                piece = value[p * members:(p + 1) * members, place * 128:(place + 1) * 128]
                send[chunk, pl.ds(start, members, stride=tiles * rows), :] = piece

    def each_gx(work):
        def some(turn, carry):
            for place in range(UNROLL):
                work(turn * UNROLL + place)
            return carry

        lax.fori_loop(0, planes // UNROLL, some, 0)

    half = slabs // 2

    def slab_at(turn):
        side = lax.rem(slab // half + 1 + turn // half, 2)
        return side * half + lax.rem(slab + turn, half)

    def other_of(step):
        return lax.rem(group + lax.rem(step, groups), groups), slab_at(step // groups)

    def push(chunk, from_ref, to_ref, sems, rsems, tgroup, tslab):
        pltpu.make_async_remote_copy(
            src_ref=at_block(from_ref, chunk, tgroup * slabs + tslab),
            dst_ref=at_block(to_ref, chunk, me),
            send_sem=sems.at[chunk],
            recv_sem=rsems.at[chunk],
            device_id=(tgroup, tslab),
            device_id_type=MESH,
        ).start()

    def push_tile(chunk, tile, tgroup, tslab):
        def at_tile(ref, member):
            start = pl.multiple_of((member * tiles + tile) * rows, 8)
            return ref.at[chunk, pl.ds(start, rows), :]

        pltpu.make_async_remote_copy(
            src_ref=at_tile(send, tgroup * slabs + tslab),
            dst_ref=at_tile(recv, me),
            send_sem=send_sem.at[chunk],
            recv_sem=recv_sem.at[chunk],
            device_id=(tgroup, tslab),
            device_id_type=MESH,
        ).start()

    def keep_own(chunk, from_ref, to_ref, rsems):
        pltpu.make_async_copy(at_block(from_ref, chunk, me), at_block(to_ref, chunk, me), rsems.at[chunk]).start()

    def spread_out(chunk, first):
        def one(step, carry):
            tgroup, tslab = other_of(step)

            @pl.when(tgroup * slabs + tslab != me)
            def _():
                push(chunk, send, recv, send_sem, recv_sem, tgroup, tslab)

            return carry

        lax.fori_loop(first, members, one, 0)
        keep_own(chunk, send, recv, recv_sem)

    def wait_all(ref, sems, chunk):
        pltpu.make_async_copy(ref.at[chunk], ref.at[chunk], sems.at[chunk]).wait()

    def share_planes(step, ref_at, send_at, recv_at):
        tgroup = lax.rem(group + step, groups)
        pltpu.make_async_remote_copy(
            src_ref=ref_at, dst_ref=ref_at, send_sem=send_at, recv_sem=recv_at,
            device_id=(tgroup, slab), device_id_type=MESH,
        ).start()

    for b in range(nbands):
        weights[group, b] = jnp.full((8, 128), occ[b].astype(jnp.float32) * (1.0 / (nbands * groups)))
    loads[1].wait()
    loads[2].wait()
    for tile in range(tiles):
        def start_one(gx, tile=tile):
            if tile < nbands:
                prepare(gx, tile)
            z_planes(0, gx, tile, tile + 1)

        each_gx(start_one)
        if tile == 0:
            pl.semaphore_wait(barrier, members - 1)

        def one(step, carry, tile=tile):
            push_tile(0, tile, *other_of(step))
            return carry

        lax.fori_loop(0, members // 2, one, 0)
    spread_out(0, members // 2)
    for step in range(1, groups):
        share_planes(step, weights.at[group], w_send.at[0], w_recv.at[0])
    for chunk in range(1, chunks):
        each_gx(lambda gx, chunk=chunk: z_planes(chunk, gx, 0, tiles))
        spread_out(chunk, 0)

    others = weights.at[pl.ds(0, groups - 1)]
    pltpu.make_async_copy(others, others, w_recv.at[0]).wait()
    pltpu.make_async_copy(others, others, w_send.at[0]).wait()

    for load in loads[3:]:
        load.wait()

    def middle(chunk, carry):
        wait_all(recv, recv_sem, chunk)
        dens[...] = jnp.zeros_like(dens)

        def build(g, carry):
            arrived = recv[chunk, pl.ds(pl.multiple_of(g * tiles * block, 8), tiles * block), :]
            arrived = arrived.reshape(slabs, tiles, rows, 128)
            high, low = split(
                jnp.concatenate([arrived[:, tile].reshape(block, 128) for tile in range(tiles)], axis=1)
            )
            for b in range(nbands):
                first = b * 128
                lh = high[:, first:first + doubled + 64]
                ll = low[:, first:first + doubled + 64]
                parts = []
                for c in range(2):
                    y = dot(lh, ty[0, b, c]) + dot(lh, ty[1, b, c]) + dot(ll, ty[0, b, c])
                    parts.append(y.reshape(slabs, rows, points))
                w = weights[g, b, 0:1, 0:1]
                for p in range(COUNT):
                    lead = p * (rows - window)
                    stacked = jnp.concatenate(
                        [part[:, lead:lead + window].reshape(slabs * window, points) for part in parts], axis=0
                    )
                    yh, yl = split(stacked)
                    field = dot(tx[0, p], yh) + dot(tx[1, p], yh) + dot(tx[0, p], yl)
                    wave[p, g * nbands + b] = field
                    dens[p] += w * (field[:points] * field[:points] + field[points:] * field[points:])
            return carry

        lax.fori_loop(0, groups, build, 0)
        potentials = []
        for p in range(COUNT):
            d = dens[p]
            outer = ext[:, pl.ds(group * own + chunk * COUNT + p, 1), :].reshape(points, points)
            potential = outer - SLATER * jnp.exp(jnp.log(d) * (1.0 / 3.0))
            potentials.append(potential)
            dens[p] = potential
        place = group * chunks + chunk
        low_rows = pl.ds(pl.multiple_of(place * COUNT * points, 8), COUNT * points)
        high_rows = pl.ds(pl.multiple_of(place * points, 8), points)
        vlow[low_rows, :] = jnp.concatenate([value[:, :128] for value in potentials], axis=0)
        vhigh[high_rows, :] = jnp.concatenate([value[:, 128:] for value in potentials], axis=1)
        for step in range(1, groups):
            share_planes(step, vlow.at[low_rows], v_send.at[0], v_recv.at[0])
            share_planes(step, vhigh.at[high_rows], v_send.at[1], v_recv.at[1])

        def back(turn, carry):
            g = lax.rem(group + turn, groups)
            sums = []
            for b in range(nbands):
                boths = []
                for p in range(COUNT):
                    potential = dens[p]
                    field = wave[p, g * nbands + b]
                    product = jnp.concatenate([field[:points] * potential, field[points:] * potential], axis=0)
                    ph, pll = split(product)
                    boths.append(dot(txb[0, p], ph) + dot(txb[1, p], ph) + dot(txb[0, p], pll))
                total = None
                for c in range(2):
                    low_rows, high_rows = [
                        both[c * slabs * window:(c + 1) * slabs * window].reshape(slabs, window, points) for both in boths
                    ]
                    cut = rows - window
                    merged = jnp.concatenate(
                        [low_rows[:, :cut], low_rows[:, cut:] + high_rows[:, :window - cut], high_rows[:, window - cut:]], axis=1
                    ).reshape(block, points)
                    mh, ml = split(merged)
                    value = dot(mh, tyb[0, b, c]) + dot(mh, tyb[1, b, c]) + dot(ml, tyb[0, b, c])
                    total = value if total is None else total + value
                sums.append(total)
            first, second = sums
            pieces = [first[:, :128], first[:, 128:] + second[:, :128], second[:, 128:]]
            sendb[chunk, pl.ds(pl.multiple_of(g * tiles * block, 8), tiles * block), :] = jnp.concatenate(
                [piece.reshape(slabs, 1, rows, 128) for piece in pieces], axis=1
            ).reshape(tiles * block, 128)

            def one(step, carry):
                tslab = slab_at(step)

                @pl.when(g * slabs + tslab != me)
                def _():
                    push(chunk, sendb, recvb, sendb_sem, recvb_sem, g, tslab)

                return carry

            lax.fori_loop(0, slabs, one, 0)
            return carry

        lax.fori_loop(0, groups, back, 0)
        keep_own(chunk, sendb, recvb, recvb_sem)
        return carry

    lax.fori_loop(0, chunks, middle, 0)

    def z_back(chunk):
        wait_all(recvb, recvb_sem, chunk)

        def one(gx):
            columns = []
            for tile in range(tiles):
                starts = [tile * rows + p * planes + gx for p in range(COUNT)]
                columns.append(jnp.concatenate(
                    [recvb[chunk, pl.ds(start, members, stride=tiles * rows), :] for start in starts], axis=0
                ))
            turned = jnp.concatenate(columns, axis=1).T
            high, low = split(turned)
            for b in range(nbands):
                total = None
                for c in range(2):
                    first = (b * 2 + c) * width
                    th, tl = high[first:first + width], low[first:first + width]
                    part = dot(th, tzb[0, chunk, c]) + dot(th, tzb[1, chunk, c]) + dot(tl, tzb[0, chunk, c])
                    total = part if total is None else total + part
                if chunk > 0:
                    total = total + out[b, gx]
                if chunk == chunks - 1:
                    index = slab * planes + gx
                    freq = jnp.where(index < width // 2, index, index - width)
                    kinetic = KINETIC * ((freq * freq).astype(jnp.float32) + square[...])
                    total = jnp.where(keep_of(gx), kinetic * coef[b, gx] + total, 0.0)
                out[b, gx] = total

        each_gx(one)

    def wait_planes(sems):
        for place, ref in enumerate((vlow, vhigh)):
            given = ref.at[pl.ds(0, (groups - 1) * (ref.shape[0] // groups))]
            pltpu.make_async_copy(given, given, sems.at[place]).wait()

    for chunk in range(chunks - 1):
        z_back(chunk)

    wait_planes(v_recv)
    spare = points - 128

    def widen(place, carry):
        value = vhigh[pl.ds(pl.multiple_of(place * points, 8), points), :]
        vwide[pl.ds(pl.multiple_of(place * COUNT * points, 8), points), :] = value
        vwide[pl.ds(pl.multiple_of((place * COUNT + 1) * points, 8), points), :] = pltpu.roll(value, spare, 1)
        return carry

    lax.fori_loop(0, groups * chunks, widen, 0)
    layers = own * groups

    def place_row(x, carry):
        first = vlow[pl.ds(x, layers, stride=points), :]
        second = vwide[pl.ds(x, layers, stride=points), :]
        pot[x] = jnp.concatenate([first, second[:, :spare]], axis=1)
        return carry

    lax.fori_loop(0, points, place_row, 0)
    z_back(chunks - 1)

    def wait_sent(ref, sems, chunk):
        sent = ref.at[chunk, pl.ds(0, (members - 1) * tiles * rows), :]
        pltpu.make_async_copy(sent, sent, sems.at[chunk]).wait()

    for chunk in range(chunks):
        wait_sent(send, send_sem, chunk)
        wait_sent(sendb, sendb_sem, chunk)
    wait_planes(v_send)


def fused_plan(coefficients, occupation, pencil_reach, external):
    nbands, planes, width, doubled = coefficients.shape
    points = 2 * width
    slabs = lax.axis_size("slab")
    groups = lax.axis_size("band")
    layers = points // slabs
    own = layers // groups
    chunks = own // COUNT
    members = groups * slabs
    rows = COUNT * planes
    lanes = nbands * doubled
    first, *rest = fused_tables(width, nbands, planes, slabs, groups, own)
    tables = [jnp.asarray(np.concatenate(split_np(first), axis=1))]
    tables += [jnp.asarray(np.stack(split_np(table))) for table in rest]
    wavenumbers = np.where(np.arange(width) < width // 2, np.arange(width), np.arange(width) - width)
    twice = np.concatenate([wavenumbers, wavenumbers])
    square = jnp.asarray((wavenumbers[:, None] ** 2 + twice[None] ** 2).astype(np.float32))
    vmem = pl.BlockSpec(memory_space=pltpu.VMEM)
    smem = pl.BlockSpec(memory_space=pltpu.SMEM)
    hbm = pl.BlockSpec(memory_space=pl.ANY)
    operands = [coefficients, pencil_reach, occupation, external, square] + tables
    bf, f32 = jnp.bfloat16, jnp.float32
    dma = pltpu.SemaphoreType.DMA
    exchange = pltpu.VMEM((chunks, members * rows * lanes // 128, 128), f32)
    mixed = pltpu.VMEM((planes, nbands * 2 * width, doubled), bf)
    return pl.pallas_call(
        functools.partial(fused_kernel, (nbands, planes, width, slabs, groups, own)),
        name="fused",
        out_shape=[
            pltpu.VMEM(coefficients.shape, f32),
            pltpu.VMEM(external.shape, f32),
        ],
        in_specs=[hbm, hbm, smem, hbm, hbm] + [hbm] * len(tables),
        out_specs=[vmem, vmem],
        scratch_shapes=[
            pltpu.VMEM(coefficients.shape, f32),
            pltpu.VMEM(pencil_reach.shape, jnp.int32),
            pltpu.VMEM(external.shape, f32),
            pltpu.VMEM(square.shape, f32),
        ] + [pltpu.VMEM(table.shape, bf) for table in tables] + [
            pltpu.VMEM((planes, width, 128), f32),
            mixed, mixed, exchange, exchange, exchange, exchange,
            pltpu.VMEM((COUNT, groups * nbands, 2 * points, points), f32),
            pltpu.VMEM((COUNT, points, points), f32),
            pltpu.VMEM((groups, nbands, 8, 128), f32),
            pltpu.VMEM((layers * points, 128), f32),
            pltpu.VMEM((groups * chunks * points, 128), f32),
            pltpu.VMEM((layers * points, 128), f32),
            dma((10,)), dma((chunks,)), dma((chunks,)), dma((chunks,)), dma((chunks,)),
            dma((2,)), dma((2,)), dma((1,)), dma((1,)),
        ],
        compiler_params=pltpu.CompilerParams(
            collective_id=0, has_side_effects=True, vmem_limit_bytes=52 * 2**20
        ),
    )(*operands)


def shards(coefficients, occupation, pencil_reach, external):
    nbands, planes, width, doubled = coefficients.shape
    slabs, groups = lax.axis_size("slab"), lax.axis_size("band")
    layers = doubled // slabs
    fits = (
        layers % (groups * COUNT) == 0 and nbands == 2 and planes == 12 and width == 96 and slabs % 2 == 0
    )
    plan = fused_plan if fits else slab_plan
    return plan(coefficients, occupation, pencil_reach, external)


def solution(mesh):
    return jax.shard_map(
        shards,
        mesh=mesh,
        in_specs=(P("band", "slab", None, None), P("band"), P("slab", None), P(None, "slab", None)),
        out_specs=(P("band", "slab", None, None), P(None, "slab", None)),
        check_vma=False,
    )
```

```python
import functools
import math

import jax
import jax.numpy as jnp
import ml_dtypes
import numpy as np
from jax import lax
from jax.experimental import pallas as pl
from jax.experimental.pallas import tpu as pltpu
from jax.sharding import PartitionSpec as P

KINETIC = 0.0005
SLATER = 0.9847
COUNT = 2
UNROLL = 3
MESH = pl.DeviceIdType.MESH


def frequency(length):
    indices = jnp.arange(length, dtype=jnp.int32)
    return jnp.where(indices < length // 2, indices, indices - length)


def inverse_table(length, extent):
    wavenumbers = frequency(length)
    positions = jnp.arange(extent, dtype=jnp.int32)
    phases = positions[:, None] * wavenumbers[None, :] % extent
    angles = phases.astype(jnp.float32) * (2.0 * math.pi / extent)
    factor = length ** (-0.5)
    cosine = jnp.cos(angles) * factor
    sine_part = jnp.sin(angles) * factor
    return jnp.stack([jnp.stack([cosine, -sine_part], 1), jnp.stack([sine_part, cosine], 1)], 0)


def forward_table(length, extent):
    wavenumbers = frequency(length)
    positions = jnp.arange(extent, dtype=jnp.int32)
    phases = wavenumbers[:, None] * positions[None, :] % extent
    angles = phases.astype(jnp.float32) * (2.0 * math.pi / extent)
    factor = length**0.5 / extent
    cosine = jnp.cos(angles) * factor
    sine_part = jnp.sin(angles) * factor
    return jnp.stack([jnp.stack([cosine, sine_part], 1), jnp.stack([-sine_part, cosine], 1)], 0)


def contract(form, left, right):
    return jnp.einsum(form, left, right, precision=lax.Precision.HIGH)


def slab_plan(coefficients, occupation, pencil_reach, external):
    nbands, planes, width, doubled = coefficients.shape
    points = 2 * width
    slabs = lax.axis_size("slab")
    layers = points // slabs
    groups = lax.axis_size("band")
    inverse = inverse_table(width, points)
    forward = forward_table(width, points)
    wavenumbers = frequency(width)
    sphere = (jnp.abs(wavenumbers)[None, None, :] <= pencil_reach[:, :, None]).astype(jnp.float32)
    sphere_full = sphere[None, :, :, None, :]
    masked = coefficients.reshape(nbands, planes, width, 2, width) * sphere_full
    along_z = contract("bxgci,onci->bxnog", masked, inverse)
    flattened = along_z.reshape(nbands, planes, points, 2 * width)
    received = lax.all_to_all(flattened, "slab", split_axis=2, concat_axis=1, tiled=True)
    columns = received.reshape(received.shape[0], width, layers, 2, width)
    spread = contract("bkzcg,oycg->bkzoy", columns, inverse)
    wavefield = contract("bkzcy,oxck->bxzoy", spread, inverse)
    squares = jnp.sum(wavefield * wavefield, axis=3)
    weights = occupation.astype(jnp.float32) / (nbands * groups)
    partial_value = contract("b,bxzy->xzy", weights, squares)
    rows_all = points * layers
    share = (rows_all + groups - 1) // groups
    flat_partial = partial_value.reshape(rows_all, points)
    density = lax.psum_scatter(flat_partial, "band", scatter_dimension=0, tiled=True)
    flat_external = external.reshape(rows_all, points)
    start_row = lax.axis_index("band") * share
    own_external = lax.dynamic_slice_in_dim(flat_external, start_row, share, 0)
    own_potential = own_external - SLATER * jnp.cbrt(density)
    gathered = lax.all_gather(own_potential, "band", axis=0, tiled=True)
    potential_all = gathered.reshape(points, layers, points)
    product = wavefield * potential_all[None, :, :, None, :]
    back_rows = contract("bxzcy,okcx->bkzoy", product, forward)
    back_y = contract("bkzcy,ogcy->bkzog", back_rows, forward).reshape(
        nbands, width, layers, 2 * width
    )
    received = lax.all_to_all(back_y, "slab", split_axis=1, concat_axis=2, tiled=True)
    blocks = received.reshape(received.shape[0], planes, points, 2, width)
    returned = contract("bxncg,ohcn->bxgoh", blocks, forward)
    plane_index = lax.axis_index("slab") * planes + jnp.arange(planes, dtype=jnp.int32)
    plane_freq = jnp.where(plane_index < width // 2, plane_index, plane_index - width)
    plane_sq = (plane_freq * plane_freq).astype(jnp.float32)
    wave_sq = (wavenumbers * wavenumbers).astype(jnp.float32)
    kinetic = KINETIC * (plane_sq[:, None, None] + wave_sq[None, :, None] + wave_sq[None, None, :])
    finished = sphere_full * (kinetic[None, :, :, None, :] * masked + returned)
    return (finished.reshape(nbands, planes, width, 2 * width), potential_all)


def split_np(table):
    high = table.astype(ml_dtypes.bfloat16)
    low = (table - high.astype(np.float64)).astype(ml_dtypes.bfloat16)
    return high, low


def split(value):
    high = value.astype(jnp.bfloat16)
    low = (value - high.astype(jnp.float32)).astype(jnp.bfloat16)
    return high, low


def dot(left, right):
    return jnp.dot(left, right, preferred_element_type=jnp.float32)


def dot_t(left, right):
    return lax.dot_general(left, right, (((1,), (1,)), ((), ())), preferred_element_type=jnp.float32)


def fused_tables(width, nbands, planes, slabs, groups, own):
    points = 2 * width
    doubled = 2 * width
    layers = points // slabs
    chunks = own // COUNT
    rows = COUNT * planes
    indices = np.arange(width)
    wave = np.where(indices < width // 2, indices, indices - width)
    phase = (np.arange(points)[:, None] * wave[None, :]) % points
    angles = phase * (2.0 * math.pi / points)
    cos, sin = np.cos(angles), np.sin(angles)
    inv = width**-0.5
    fwd = width**0.5 / points
    z_of = np.array(
        [
            [
                s * layers + g * own + part * COUNT + p
                for p in range(COUNT)
                for g in range(groups)
                for s in range(slabs)
            ]
            for part in range(chunks)
        ]
    )
    tz = np.concatenate([cos, -sin], 1)[z_of] * inv
    span = doubled + 64
    ty = np.zeros((nbands, 2, span, points))
    tyb = np.zeros((nbands, 2, points, span))
    for b in range(nbands):
        shift = b * doubled - b * 128
        ty[b, 0, shift:shift + width] = cos.T * inv
        ty[b, 0, shift + width:shift + doubled] = -sin.T * inv
        ty[b, 1, shift:shift + width] = sin.T * inv
        ty[b, 1, shift + width:shift + doubled] = cos.T * inv
        tyb[b, 0, :, shift:shift + width] = cos * fwd
        tyb[b, 0, :, shift + width:shift + doubled] = -sin * fwd
        tyb[b, 1, :, shift:shift + width] = sin * fwd
        tyb[b, 1, :, shift + width:shift + doubled] = cos * fwd
    window = 16
    tx = np.zeros((COUNT, 2, points, 2, slabs, window))
    txb = np.zeros((COUNT, 2, slabs, window, 2, points))
    for p in range(COUNT):
        first = p * planes - p * (rows - window)
        put = slice(first, first + planes)
        c3 = cos.reshape(points, slabs, planes)
        s3 = sin.reshape(points, slabs, planes)
        tx[p, 0, :, 0][:, :, put] = c3 * inv
        tx[p, 0, :, 1][:, :, put] = -s3 * inv
        tx[p, 1, :, 0][:, :, put] = s3 * inv
        tx[p, 1, :, 1][:, :, put] = c3 * inv
        ct, st = c3.transpose(1, 2, 0), s3.transpose(1, 2, 0)
        txb[p, 0][:, put, 0] = ct * fwd
        txb[p, 0][:, put, 1] = st * fwd
        txb[p, 1][:, put, 0] = -st * fwd
        txb[p, 1][:, put, 1] = ct * fwd
    tx = tx.reshape(COUNT, 2 * points, 2 * slabs * window)
    txb = txb.reshape(COUNT, 2 * slabs * window, 2 * points)
    tzb = np.stack([np.concatenate([cos, -sin], 1)[z_of], np.concatenate([sin, cos], 1)[z_of]], 1) * fwd
    return tz, ty, tx, txb, tyb, tzb


def keep_rows(column, gx, width):
    lane = lax.rem(lax.broadcasted_iota(jnp.int32, (1, 2 * width), 1), width)
    absk = jnp.where(lane < width // 2, lane, width - lane).astype(jnp.float32)
    return absk <= column[gx][:, 0:1]


def z_back_one(landed, chunk, gx, table, part, nbands, width, members, rows, planes):
    tiles = nbands * 2 * width // 128
    columns = []
    for tile in range(tiles):
        starts = [tile * rows + p * planes + gx for p in range(COUNT)]
        columns.append(jnp.concatenate(
            [landed[chunk, pl.ds(start, members, stride=tiles * rows), :] for start in starts], axis=0
        ))
    high, low = split(jnp.concatenate(columns, axis=1))
    turned = jnp.concatenate([high, high, low], axis=0).T
    values = []
    for b in range(nbands):
        total = None
        for c in range(2):
            first = (b * 2 + c) * width
            part_sum = dot(turned[first:first + width], table[part, c])
            total = part_sum if total is None else total + part_sum
        values.append(total)
    return values


def finish_kernel(sizes, start, pot, landed, column, table, out_hbm, pot_hbm, out, out_sem, pot_sem):
    nbands, planes, width, members = sizes
    whole = pltpu.make_async_copy(pot, pot_hbm, pot_sem)
    whole.start()
    chunk = landed.shape[0] - 1

    def some(turn, carry):
        for gx in [turn * UNROLL + place for place in range(UNROLL)]:
            values = z_back_one(landed, chunk, gx, table, 0, nbands, width, members, COUNT * planes, planes)
            for b in range(nbands):
                out[b, gx] = start[b, gx] + jnp.where(keep_rows(column, gx, width), values[b], 0.0)
                pltpu.make_async_copy(out.at[b, gx], out_hbm.at[b, gx], out_sem).start()
        return carry

    lax.fori_loop(0, planes // UNROLL, some, 0)
    pltpu.make_async_copy(out, out_hbm, out_sem).wait()
    whole.wait()


def fused_kernel(
    sizes,
    coef_hbm, reach_hbm, occ, ext_hbm, square_hbm, tz_hbm, ty_hbm, tx_hbm, txb_hbm, tyb_hbm, tzb_hbm,
    out, pot, recvb, column, last_table,
    coef, reach, ext, square, tz, ty, tx, txb, tyb, tzb,
    xh, xl, send, recv, sendb, wave, dens, weights, vlow, vhigh, vwide,
    load_sem, send_sem, recv_sem, sendb_sem, recvb_sem, v_send, v_recv, w_send, w_recv,
):
    nbands, planes, width, slabs, groups, own = sizes
    points = 2 * width
    doubled = 2 * width
    chunks = own // COUNT
    members = groups * slabs
    rows = COUNT * planes
    block = slabs * rows
    tiles = nbands * doubled // 128
    window = 16
    zs = COUNT * members
    group = lax.axis_index("band")
    slab = lax.axis_index("slab")
    me = group * slabs + slab

    def at_block(ref, chunk, member):
        return ref.at[chunk, pl.ds(pl.multiple_of(member * tiles * rows, 8), tiles * rows), :]

    loads = [
        pltpu.make_async_copy(source, target, load_sem.at[place])
        for place, (source, target) in enumerate([
            (reach_hbm, reach), (tz_hbm, tz), (coef_hbm, coef),
            (ty_hbm, ty), (tx_hbm, tx), (ext_hbm, ext), (txb_hbm, txb), (tyb_hbm, tyb), (tzb_hbm, tzb),
            (square_hbm, square),
        ])
    ]
    for load in loads:
        load.start()

    barrier = pltpu.get_barrier_semaphore()

    def greet(step, carry):
        other = lax.rem(me + step, members)
        pl.semaphore_signal(barrier, inc=1, device_id=(other // slabs, lax.rem(other, slabs)), device_id_type=MESH)
        return carry

    lax.fori_loop(1, members, greet, 0)

    loads[0].wait()
    turned_reach = reach[...].astype(jnp.float32).T
    for gx in range(planes):
        column[gx] = jnp.broadcast_to(turned_reach[:, gx:gx + 1], (width, 128))

    def keep_of(gx):
        return keep_rows(column, gx, width)

    def prepare(gx, b):
        value = jnp.where(keep_of(gx), coef[b, gx], 0.0)
        turned = jnp.concatenate([value[:, width:], -value[:, :width]], axis=1)
        high, low = split(jnp.concatenate([value, turned], axis=0))
        xh[gx, b * doubled:(b + 1) * doubled] = high
        xl[gx, b * doubled:(b + 1) * doubled] = low

    def z_planes(chunk, gx, first_tile, last_tile):
        lanes = slice(first_tile * 128, last_tile * 128)
        both = dot_t(tz[chunk], xh[gx, lanes])
        value = both[:zs] + both[zs:] + dot_t(tz[chunk, :zs], xl[gx, lanes])
        for p in range(COUNT):
            for tile in range(first_tile, last_tile):
                start = tile * rows + p * planes + gx
                place = tile - first_tile
                piece = value[p * members:(p + 1) * members, place * 128:(place + 1) * 128]
                send[chunk, pl.ds(start, members, stride=tiles * rows), :] = piece

    def each_gx(work):
        def some(turn, carry):
            for place in range(UNROLL):
                work(turn * UNROLL + place)
            return carry

        lax.fori_loop(0, planes // UNROLL, some, 0)

    half = slabs // 2

    def slab_at(turn):
        side = lax.rem(slab // half + 1 + turn // half, 2)
        return side * half + lax.rem(slab + turn, half)

    def other_of(step):
        return lax.rem(group + lax.rem(step, groups), groups), slab_at(step // groups)

    def push(chunk, from_ref, to_ref, sems, rsems, tgroup, tslab):
        pltpu.make_async_remote_copy(
            src_ref=at_block(from_ref, chunk, tgroup * slabs + tslab),
            dst_ref=at_block(to_ref, chunk, me),
            send_sem=sems.at[chunk],
            recv_sem=rsems.at[chunk],
            device_id=(tgroup, tslab),
            device_id_type=MESH,
        ).start()

    def push_tile(chunk, tile, tgroup, tslab):
        def at_tile(ref, member):
            start = pl.multiple_of((member * tiles + tile) * rows, 8)
            return ref.at[chunk, pl.ds(start, rows), :]

        pltpu.make_async_remote_copy(
            src_ref=at_tile(send, tgroup * slabs + tslab),
            dst_ref=at_tile(recv, me),
            send_sem=send_sem.at[chunk],
            recv_sem=recv_sem.at[chunk],
            device_id=(tgroup, tslab),
            device_id_type=MESH,
        ).start()

    def keep_own(chunk, from_ref, to_ref, rsems):
        pltpu.make_async_copy(at_block(from_ref, chunk, me), at_block(to_ref, chunk, me), rsems.at[chunk]).start()

    def spread_out(chunk, first):
        def one(step, carry):
            tgroup, tslab = other_of(step)

            @pl.when(tgroup * slabs + tslab != me)
            def _():
                push(chunk, send, recv, send_sem, recv_sem, tgroup, tslab)

            return carry

        lax.fori_loop(first, members, one, 0)
        keep_own(chunk, send, recv, recv_sem)

    def wait_all(ref, sems, chunk):
        pltpu.make_async_copy(ref.at[chunk], ref.at[chunk], sems.at[chunk]).wait()

    def share_planes(step, ref_at, send_at, recv_at):
        tgroup = lax.rem(group + step, groups)
        pltpu.make_async_remote_copy(
            src_ref=ref_at, dst_ref=ref_at, send_sem=send_at, recv_sem=recv_at,
            device_id=(tgroup, slab), device_id_type=MESH,
        ).start()

    for b in range(nbands):
        weights[group, b] = jnp.full((8, 128), occ[b].astype(jnp.float32) * (1.0 / (nbands * groups)))
    loads[1].wait()
    loads[2].wait()
    for tile in range(tiles):
        def start_one(gx, tile=tile):
            if tile < nbands:
                prepare(gx, tile)
            z_planes(0, gx, tile, tile + 1)

        each_gx(start_one)
        if tile == 0:
            pl.semaphore_wait(barrier, members - 1)

        def one(step, carry, tile=tile):
            push_tile(0, tile, *other_of(step))
            return carry

        lax.fori_loop(0, members // 2, one, 0)
    spread_out(0, members // 2)
    for step in range(1, groups):
        share_planes(step, weights.at[group], w_send.at[0], w_recv.at[0])
    for chunk in range(1, chunks):
        each_gx(lambda gx, chunk=chunk: z_planes(chunk, gx, 0, tiles))
        spread_out(chunk, 0)

    others = weights.at[pl.ds(0, groups - 1)]
    pltpu.make_async_copy(others, others, w_recv.at[0]).wait()
    pltpu.make_async_copy(others, others, w_send.at[0]).wait()

    for load in loads[3:]:
        load.wait()

    def middle(chunk, carry):
        wait_all(recv, recv_sem, chunk)
        dens[...] = jnp.zeros_like(dens)

        def build(g, carry):
            arrived = recv[chunk, pl.ds(pl.multiple_of(g * tiles * block, 8), tiles * block), :]
            arrived = arrived.reshape(slabs, tiles, rows, 128)
            high, low = split(
                jnp.concatenate([arrived[:, tile].reshape(block, 128) for tile in range(tiles)], axis=1)
            )
            for b in range(nbands):
                first = b * 128
                lh = high[:, first:first + doubled + 64]
                ll = low[:, first:first + doubled + 64]
                parts = []
                for c in range(2):
                    y = dot(lh, ty[0, b, c]) + dot(lh, ty[1, b, c]) + dot(ll, ty[0, b, c])
                    parts.append(y.reshape(slabs, rows, points))
                w = weights[g, b, 0:1, 0:1]
                for p in range(COUNT):
                    lead = p * (rows - window)
                    stacked = jnp.concatenate(
                        [part[:, lead:lead + window].reshape(slabs * window, points) for part in parts], axis=0
                    )
                    yh, yl = split(stacked)
                    field = dot(tx[0, p], yh) + dot(tx[1, p], yh) + dot(tx[0, p], yl)
                    wave[p, g * nbands + b] = field
                    dens[p] += w * (field[:points] * field[:points] + field[points:] * field[points:])
            return carry

        lax.fori_loop(0, groups, build, 0)
        potentials = []
        for p in range(COUNT):
            d = dens[p]
            outer = ext[:, pl.ds(group * own + chunk * COUNT + p, 1), :].reshape(points, points)
            potential = outer - SLATER * jnp.exp(jnp.log(d) * (1.0 / 3.0))
            potentials.append(potential)
            dens[p] = potential
        place = group * chunks + chunk
        low_rows = pl.ds(pl.multiple_of(place * COUNT * points, 8), COUNT * points)
        high_rows = pl.ds(pl.multiple_of(place * points, 8), points)
        vlow[low_rows, :] = jnp.concatenate([value[:, :128] for value in potentials], axis=0)
        vhigh[high_rows, :] = jnp.concatenate([value[:, 128:] for value in potentials], axis=1)
        for step in range(1, groups):
            share_planes(step, vlow.at[low_rows], v_send.at[0], v_recv.at[0])
            share_planes(step, vhigh.at[high_rows], v_send.at[1], v_recv.at[1])

        def back(turn, carry):
            g = lax.rem(group + turn, groups)
            sums = []
            for b in range(nbands):
                boths = []
                for p in range(COUNT):
                    potential = dens[p]
                    field = wave[p, g * nbands + b]
                    product = jnp.concatenate([field[:points] * potential, field[points:] * potential], axis=0)
                    ph, pll = split(product)
                    boths.append(dot(txb[0, p], ph) + dot(txb[1, p], ph) + dot(txb[0, p], pll))
                total = None
                for c in range(2):
                    low_rows, high_rows = [
                        both[c * slabs * window:(c + 1) * slabs * window].reshape(slabs, window, points) for both in boths
                    ]
                    cut = rows - window
                    merged = jnp.concatenate(
                        [low_rows[:, :cut], low_rows[:, cut:] + high_rows[:, :window - cut], high_rows[:, window - cut:]], axis=1
                    ).reshape(block, points)
                    mh, ml = split(merged)
                    value = dot(mh, tyb[0, b, c]) + dot(mh, tyb[1, b, c]) + dot(ml, tyb[0, b, c])
                    total = value if total is None else total + value
                sums.append(total)
            first, second = sums
            pieces = [first[:, :128], first[:, 128:] + second[:, :128], second[:, 128:]]
            sendb[chunk, pl.ds(pl.multiple_of(g * tiles * block, 8), tiles * block), :] = jnp.concatenate(
                [piece.reshape(slabs, 1, rows, 128) for piece in pieces], axis=1
            ).reshape(tiles * block, 128)

            def one(step, carry):
                tslab = slab_at(step)

                @pl.when(g * slabs + tslab != me)
                def _():
                    push(chunk, sendb, recvb, sendb_sem, recvb_sem, g, tslab)

                return carry

            lax.fori_loop(0, slabs, one, 0)
            return carry

        lax.fori_loop(0, groups, back, 0)
        keep_own(chunk, sendb, recvb, recvb_sem)
        return carry

    lax.fori_loop(0, chunks, middle, 0)

    def z_back(chunk):
        wait_all(recvb, recvb_sem, chunk)

        def one(gx):
            values = z_back_one(recvb, chunk, gx, tzb, chunk, nbands, width, members, rows, planes)
            for b in range(nbands):
                total = values[b]
                if chunk > 0:
                    total = total + out[b, gx]
                if chunk == chunks - 2:
                    index = slab * planes + gx
                    freq = jnp.where(index < width // 2, index, index - width)
                    kinetic = KINETIC * ((freq * freq).astype(jnp.float32) + square[...])
                    total = jnp.where(keep_of(gx), kinetic * coef[b, gx] + total, 0.0)
                out[b, gx] = total

        each_gx(one)

    def wait_planes(sems):
        for place, ref in enumerate((vlow, vhigh)):
            given = ref.at[pl.ds(0, (groups - 1) * (ref.shape[0] // groups))]
            pltpu.make_async_copy(given, given, sems.at[place]).wait()

    for chunk in range(chunks - 1):
        z_back(chunk)

    wait_planes(v_recv)
    spare = points - 128

    def widen(place, carry):
        value = vhigh[pl.ds(pl.multiple_of(place * points, 8), points), :]
        vwide[pl.ds(pl.multiple_of(place * COUNT * points, 8), points), :] = value
        vwide[pl.ds(pl.multiple_of((place * COUNT + 1) * points, 8), points), :] = pltpu.roll(value, spare, 1)
        return carry

    lax.fori_loop(0, groups * chunks, widen, 0)
    layers = own * groups

    def place_row(x, carry):
        first = vlow[pl.ds(x, layers, stride=points), :]
        second = vwide[pl.ds(x, layers, stride=points), :]
        pot[x] = jnp.concatenate([first, second[:, :spare]], axis=1)
        return carry

    lax.fori_loop(0, points, place_row, 0)
    last_table[0] = tzb[chunks - 1]
    wait_all(recvb, recvb_sem, chunks - 1)

    def wait_sent(ref, sems, chunk):
        sent = ref.at[chunk, pl.ds(0, (members - 1) * tiles * rows), :]
        pltpu.make_async_copy(sent, sent, sems.at[chunk]).wait()

    for chunk in range(chunks):
        wait_sent(send, send_sem, chunk)
        wait_sent(sendb, sendb_sem, chunk)
    wait_planes(v_send)


def fused_plan(coefficients, occupation, pencil_reach, external):
    nbands, planes, width, doubled = coefficients.shape
    points = 2 * width
    slabs = lax.axis_size("slab")
    groups = lax.axis_size("band")
    layers = points // slabs
    own = layers // groups
    chunks = own // COUNT
    members = groups * slabs
    rows = COUNT * planes
    lanes = nbands * doubled
    first, *rest, last = fused_tables(width, nbands, planes, slabs, groups, own)
    tables = [jnp.asarray(np.concatenate(split_np(first), axis=1))]
    tables += [jnp.asarray(np.stack(split_np(table))) for table in rest]
    high, low = split_np(last)
    tables += [jnp.asarray(np.concatenate([high, low, high], axis=2))]
    wavenumbers = np.where(np.arange(width) < width // 2, np.arange(width), np.arange(width) - width)
    twice = np.concatenate([wavenumbers, wavenumbers])
    square = jnp.asarray((wavenumbers[:, None] ** 2 + twice[None] ** 2).astype(np.float32))
    vmem = pl.BlockSpec(memory_space=pltpu.VMEM)
    smem = pl.BlockSpec(memory_space=pltpu.SMEM)
    hbm = pl.BlockSpec(memory_space=pl.ANY)
    operands = [coefficients, pencil_reach, occupation, external, square] + tables
    bf, f32 = jnp.bfloat16, jnp.float32
    dma = pltpu.SemaphoreType.DMA
    exchange = pltpu.VMEM((chunks, members * rows * lanes // 128, 128), f32)
    mixed = pltpu.VMEM((planes, nbands * 2 * width, doubled), bf)
    results = [
        pltpu.VMEM(coefficients.shape, f32),
        pltpu.VMEM(external.shape, f32),
        exchange,
        pltpu.VMEM((planes, width, 128), f32),
        pltpu.VMEM((1,) + tables[-1].shape[1:], bf),
    ]
    gathered = pl.pallas_call(
        functools.partial(fused_kernel, (nbands, planes, width, slabs, groups, own)),
        name="fused",
        out_shape=results,
        in_specs=[hbm, hbm, smem, hbm, hbm] + [hbm] * len(tables),
        out_specs=[vmem] * len(results),
        scratch_shapes=[
            pltpu.VMEM(coefficients.shape, f32),
            pltpu.VMEM(pencil_reach.shape, jnp.int32),
            pltpu.VMEM(external.shape, f32),
            pltpu.VMEM(square.shape, f32),
        ] + [pltpu.VMEM(table.shape, bf) for table in tables] + [
            mixed, mixed, exchange, exchange, exchange,
            pltpu.VMEM((COUNT, groups * nbands, 2 * points, points), f32),
            pltpu.VMEM((COUNT, points, points), f32),
            pltpu.VMEM((groups, nbands, 8, 128), f32),
            pltpu.VMEM((layers * points, 128), f32),
            pltpu.VMEM((groups * chunks * points, 128), f32),
            pltpu.VMEM((layers * points, 128), f32),
            dma((10,)), dma((chunks,)), dma((chunks,)), dma((chunks,)), dma((chunks,)),
            dma((2,)), dma((2,)), dma((1,)), dma((1,)),
        ],
        compiler_params=pltpu.CompilerParams(
            collective_id=0, has_side_effects=True, vmem_limit_bytes=46 * 2**20
        ),
    )(*operands)
    return pl.pallas_call(
        functools.partial(finish_kernel, (nbands, planes, width, members)),
        name="finish",
        out_shape=[
            jax.ShapeDtypeStruct(coefficients.shape, f32),
            jax.ShapeDtypeStruct(external.shape, f32),
        ],
        in_specs=[vmem] * len(results),
        out_specs=[hbm, hbm],
        scratch_shapes=[pltpu.VMEM(coefficients.shape, f32), dma, dma],
        compiler_params=pltpu.CompilerParams(vmem_limit_bytes=12 * 2**20),
    )(*gathered)


def shards(coefficients, occupation, pencil_reach, external):
    nbands, planes, width, doubled = coefficients.shape
    slabs, groups = lax.axis_size("slab"), lax.axis_size("band")
    layers = doubled // slabs
    fits = (
        layers % (groups * COUNT) == 0 and layers > groups * COUNT and nbands == 2 and planes == 12 and width == 96 and slabs % 2 == 0
    )
    plan = fused_plan if fits else slab_plan
    return plan(coefficients, occupation, pencil_reach, external)


def solution(mesh):
    return jax.shard_map(
        shards,
        mesh=mesh,
        in_specs=(P("band", "slab", None, None), P("band"), P("slab", None), P(None, "slab", None)),
        out_specs=(P("band", "slab", None, None), P(None, "slab", None)),
        check_vma=False,
    )
```

```python
import functools
import math

import jax
import jax.numpy as jnp
import ml_dtypes
import numpy as np
from jax import lax
from jax.experimental import pallas as pl
from jax.experimental.pallas import tpu as pltpu
from jax.sharding import PartitionSpec as P

KINETIC = 0.0005
SLATER = 0.9847
COUNT = 2
UNROLL = 3
MESH = pl.DeviceIdType.MESH


def frequency(length):
    indices = jnp.arange(length, dtype=jnp.int32)
    return jnp.where(indices < length // 2, indices, indices - length)


def inverse_table(length, extent):
    wavenumbers = frequency(length)
    positions = jnp.arange(extent, dtype=jnp.int32)
    phases = positions[:, None] * wavenumbers[None, :] % extent
    angles = phases.astype(jnp.float32) * (2.0 * math.pi / extent)
    factor = length ** (-0.5)
    cosine = jnp.cos(angles) * factor
    sine_part = jnp.sin(angles) * factor
    return jnp.stack([jnp.stack([cosine, -sine_part], 1), jnp.stack([sine_part, cosine], 1)], 0)


def forward_table(length, extent):
    wavenumbers = frequency(length)
    positions = jnp.arange(extent, dtype=jnp.int32)
    phases = wavenumbers[:, None] * positions[None, :] % extent
    angles = phases.astype(jnp.float32) * (2.0 * math.pi / extent)
    factor = length**0.5 / extent
    cosine = jnp.cos(angles) * factor
    sine_part = jnp.sin(angles) * factor
    return jnp.stack([jnp.stack([cosine, sine_part], 1), jnp.stack([-sine_part, cosine], 1)], 0)


def contract(form, left, right):
    return jnp.einsum(form, left, right, precision=lax.Precision.HIGH)


def slab_plan(coefficients, occupation, pencil_reach, external):
    nbands, planes, width, doubled = coefficients.shape
    points = 2 * width
    slabs = lax.axis_size("slab")
    layers = points // slabs
    groups = lax.axis_size("band")
    inverse = inverse_table(width, points)
    forward = forward_table(width, points)
    wavenumbers = frequency(width)
    sphere = (jnp.abs(wavenumbers)[None, None, :] <= pencil_reach[:, :, None]).astype(jnp.float32)
    sphere_full = sphere[None, :, :, None, :]
    masked = coefficients.reshape(nbands, planes, width, 2, width) * sphere_full
    along_z = contract("bxgci,onci->bxnog", masked, inverse)
    flattened = along_z.reshape(nbands, planes, points, 2 * width)
    received = lax.all_to_all(flattened, "slab", split_axis=2, concat_axis=1, tiled=True)
    columns = received.reshape(received.shape[0], width, layers, 2, width)
    spread = contract("bkzcg,oycg->bkzoy", columns, inverse)
    wavefield = contract("bkzcy,oxck->bxzoy", spread, inverse)
    squares = jnp.sum(wavefield * wavefield, axis=3)
    weights = occupation.astype(jnp.float32) / (nbands * groups)
    partial_value = contract("b,bxzy->xzy", weights, squares)
    rows_all = points * layers
    share = (rows_all + groups - 1) // groups
    flat_partial = partial_value.reshape(rows_all, points)
    density = lax.psum_scatter(flat_partial, "band", scatter_dimension=0, tiled=True)
    flat_external = external.reshape(rows_all, points)
    start_row = lax.axis_index("band") * share
    own_external = lax.dynamic_slice_in_dim(flat_external, start_row, share, 0)
    own_potential = own_external - SLATER * jnp.cbrt(density)
    gathered = lax.all_gather(own_potential, "band", axis=0, tiled=True)
    potential_all = gathered.reshape(points, layers, points)
    product = wavefield * potential_all[None, :, :, None, :]
    back_rows = contract("bxzcy,okcx->bkzoy", product, forward)
    back_y = contract("bkzcy,ogcy->bkzog", back_rows, forward).reshape(
        nbands, width, layers, 2 * width
    )
    received = lax.all_to_all(back_y, "slab", split_axis=1, concat_axis=2, tiled=True)
    blocks = received.reshape(received.shape[0], planes, points, 2, width)
    returned = contract("bxncg,ohcn->bxgoh", blocks, forward)
    plane_index = lax.axis_index("slab") * planes + jnp.arange(planes, dtype=jnp.int32)
    plane_freq = jnp.where(plane_index < width // 2, plane_index, plane_index - width)
    plane_sq = (plane_freq * plane_freq).astype(jnp.float32)
    wave_sq = (wavenumbers * wavenumbers).astype(jnp.float32)
    kinetic = KINETIC * (plane_sq[:, None, None] + wave_sq[None, :, None] + wave_sq[None, None, :])
    finished = sphere_full * (kinetic[None, :, :, None, :] * masked + returned)
    return (finished.reshape(nbands, planes, width, 2 * width), potential_all)


def split_np(table):
    high = table.astype(ml_dtypes.bfloat16)
    low = (table - high.astype(np.float64)).astype(ml_dtypes.bfloat16)
    return high, low


def split(value):
    high = value.astype(jnp.bfloat16)
    low = (value - high.astype(jnp.float32)).astype(jnp.bfloat16)
    return high, low


def dot(left, right):
    return jnp.dot(left, right, preferred_element_type=jnp.float32)


def dot_t(left, right):
    return lax.dot_general(left, right, (((1,), (1,)), ((), ())), preferred_element_type=jnp.float32)


def fused_tables(width, nbands, planes, slabs, groups, own):
    points = 2 * width
    doubled = 2 * width
    layers = points // slabs
    chunks = own // COUNT
    rows = COUNT * planes
    indices = np.arange(width)
    wave = np.where(indices < width // 2, indices, indices - width)
    phase = (np.arange(points)[:, None] * wave[None, :]) % points
    angles = phase * (2.0 * math.pi / points)
    cos, sin = np.cos(angles), np.sin(angles)
    inv = width**-0.5
    fwd = width**0.5 / points
    z_of = np.array(
        [
            [
                s * layers + g * own + part * COUNT + p
                for p in range(COUNT)
                for g in range(groups)
                for s in range(slabs)
            ]
            for part in range(chunks)
        ]
    )
    tz = np.concatenate([cos, -sin], 1)[z_of] * inv
    span = doubled + 64
    ty = np.zeros((nbands, 2, span, points))
    tyb = np.zeros((nbands, 2, points, span))
    for b in range(nbands):
        shift = b * doubled - b * 128
        ty[b, 0, shift:shift + width] = cos.T * inv
        ty[b, 0, shift + width:shift + doubled] = -sin.T * inv
        ty[b, 1, shift:shift + width] = sin.T * inv
        ty[b, 1, shift + width:shift + doubled] = cos.T * inv
        tyb[b, 0, :, shift:shift + width] = cos * fwd
        tyb[b, 0, :, shift + width:shift + doubled] = -sin * fwd
        tyb[b, 1, :, shift:shift + width] = sin * fwd
        tyb[b, 1, :, shift + width:shift + doubled] = cos * fwd
    window = 16
    tx = np.zeros((COUNT, 2, points, 2, slabs, window))
    txb = np.zeros((COUNT, 2, slabs, window, 2, points))
    for p in range(COUNT):
        first = p * planes - p * (rows - window)
        put = slice(first, first + planes)
        c3 = cos.reshape(points, slabs, planes)
        s3 = sin.reshape(points, slabs, planes)
        tx[p, 0, :, 0][:, :, put] = c3 * inv
        tx[p, 0, :, 1][:, :, put] = -s3 * inv
        tx[p, 1, :, 0][:, :, put] = s3 * inv
        tx[p, 1, :, 1][:, :, put] = c3 * inv
        ct, st = c3.transpose(1, 2, 0), s3.transpose(1, 2, 0)
        txb[p, 0][:, put, 0] = ct * fwd
        txb[p, 0][:, put, 1] = st * fwd
        txb[p, 1][:, put, 0] = -st * fwd
        txb[p, 1][:, put, 1] = ct * fwd
    tx = tx.reshape(COUNT, 2 * points, 2 * slabs * window)
    txb = txb.reshape(COUNT, 2 * slabs * window, 2 * points)
    tzb = np.stack([np.concatenate([cos, -sin], 1)[z_of], np.concatenate([sin, cos], 1)[z_of]], 1) * fwd
    return tz, ty, tx, txb, tyb, tzb


def keep_rows(column, gx, width, gy=slice(None)):
    lane = lax.rem(lax.broadcasted_iota(jnp.int32, (1, 2 * width), 1), width)
    absk = jnp.where(lane < width // 2, lane, width - lane).astype(jnp.float32)
    return absk <= column[gx, gy][:, 0:1]


def z_back_one(landed, chunk, gx, table, part, nbands, width, members, rows, planes):
    tiles = nbands * 2 * width // 128
    columns = []
    for tile in range(tiles):
        starts = [tile * rows + p * planes + gx for p in range(COUNT)]
        columns.append(jnp.concatenate(
            [landed[chunk, pl.ds(start, members, stride=tiles * rows), :] for start in starts], axis=0
        ))
    high, low = split(jnp.concatenate(columns, axis=1))
    turned = jnp.concatenate([high, high, low], axis=0).T
    values = []
    for b in range(nbands):
        total = None
        for c in range(2):
            first = (b * 2 + c) * width
            part_sum = dot(turned[first:first + width], table[part, c])
            total = part_sum if total is None else total + part_sum
        values.append(total)
    return values


def finish_kernel(sizes, start, pot, landed, column, table, out_hbm, pot_hbm, out, out_sem, pot_sem):
    nbands, planes, width, members = sizes
    whole = pltpu.make_async_copy(pot, pot_hbm, pot_sem)
    whole.start()
    chunk = landed.shape[0] - 1

    def some(turn, carry):
        for gx in [turn * UNROLL + place for place in range(UNROLL)]:
            values = z_back_one(landed, chunk, gx, table, 0, nbands, width, members, COUNT * planes, planes)
            for b in range(nbands):
                out[b, gx] = start[b, gx] + jnp.where(keep_rows(column, gx, width), values[b], 0.0)
                pltpu.make_async_copy(out.at[b, gx], out_hbm.at[b, gx], out_sem).start()
        return carry

    lax.fori_loop(0, planes // UNROLL, some, 0)
    pltpu.make_async_copy(out, out_hbm, out_sem).wait()
    whole.wait()


def fused_kernel(
    sizes,
    coef_hbm, reach_hbm, occ, ext_hbm, square_hbm, tz_hbm, ty_hbm, tx_hbm, txb_hbm, tyb_hbm, tzb_hbm,
    out, pot, recvb, column, last_table,
    coef, reach, ext, square, tz, ty, tx, txb, tyb, tzb,
    xh, xl, send, recv, sendb, wave, dens, weights, vlow, vhigh, vwide,
    load_sem, send_sem, recv_sem, sendb_sem, recvb_sem, v_send, v_recv, w_send, w_recv,
):
    nbands, planes, width, slabs, groups, own = sizes
    points = 2 * width
    doubled = 2 * width
    chunks = own // COUNT
    members = groups * slabs
    rows = COUNT * planes
    block = slabs * rows
    tiles = nbands * doubled // 128
    window = 16
    zs = COUNT * members
    group = lax.axis_index("band")
    slab = lax.axis_index("slab")
    me = group * slabs + slab

    def at_block(ref, chunk, member):
        return ref.at[chunk, pl.ds(pl.multiple_of(member * tiles * rows, 8), tiles * rows), :]

    loads = [
        pltpu.make_async_copy(source, target, load_sem.at[place])
        for place, (source, target) in enumerate([
            (reach_hbm, reach), (coef_hbm.at[0], coef.at[0]), (tz_hbm, tz), (coef_hbm.at[1], coef.at[1]),
            (ty_hbm, ty), (tx_hbm, tx), (ext_hbm, ext), (txb_hbm, txb), (tyb_hbm, tyb), (tzb_hbm, tzb),
            (square_hbm, square),
        ])
    ]
    for load in loads:
        load.start()

    barrier = pltpu.get_barrier_semaphore()

    def greet(step, carry):
        other = lax.rem(me + step, members)
        pl.semaphore_signal(barrier, inc=1, device_id=(other // slabs, lax.rem(other, slabs)), device_id_type=MESH)
        return carry

    lax.fori_loop(1, members, greet, 0)

    loads[0].wait()
    turned_reach = reach[...].astype(jnp.float32).T
    for gx in range(planes):
        column[gx] = jnp.broadcast_to(turned_reach[:, gx:gx + 1], (width, 128))

    def keep_of(gx):
        return keep_rows(column, gx, width)

    def prepare(gx, tile):
        for b in range(nbands):
            for c in range(2):
                base = (b * 2 + c) * width
                first, last = max(base, tile * 128), min(base + width, (tile + 1) * 128)
                if first >= last:
                    continue
                gy = slice(first - base, last - base)
                value = jnp.where(keep_rows(column, gx, width, gy), coef[b, gx, gy], 0.0)
                if c == 1:
                    value = jnp.concatenate([value[:, width:], -value[:, :width]], axis=1)
                high, low = split(value)
                xh[gx, first:last] = high
                xl[gx, first:last] = low

    def z_planes(chunk, gx, first_tile, last_tile):
        lanes = slice(first_tile * 128, last_tile * 128)
        both = dot_t(tz[chunk], xh[gx, lanes])
        value = both[:zs] + both[zs:] + dot_t(tz[chunk, :zs], xl[gx, lanes])
        for p in range(COUNT):
            for tile in range(first_tile, last_tile):
                start = tile * rows + p * planes + gx
                place = tile - first_tile
                piece = value[p * members:(p + 1) * members, place * 128:(place + 1) * 128]
                send[chunk, pl.ds(start, members, stride=tiles * rows), :] = piece

    def each_gx(work):
        def some(turn, carry):
            for place in range(UNROLL):
                work(turn * UNROLL + place)
            return carry

        lax.fori_loop(0, planes // UNROLL, some, 0)

    half = slabs // 2

    def slab_at(turn):
        side = lax.rem(slab // half + 1 + turn // half, 2)
        return side * half + lax.rem(slab + turn, half)

    def other_of(step):
        return lax.rem(group + lax.rem(step, groups), groups), slab_at(step // groups)

    def push(chunk, from_ref, to_ref, sems, rsems, tgroup, tslab):
        pltpu.make_async_remote_copy(
            src_ref=at_block(from_ref, chunk, tgroup * slabs + tslab),
            dst_ref=at_block(to_ref, chunk, me),
            send_sem=sems.at[chunk],
            recv_sem=rsems.at[chunk],
            device_id=(tgroup, tslab),
            device_id_type=MESH,
        ).start()

    def push_tile(chunk, tile, tgroup, tslab):
        def at_tile(ref, member):
            start = pl.multiple_of((member * tiles + tile) * rows, 8)
            return ref.at[chunk, pl.ds(start, rows), :]

        pltpu.make_async_remote_copy(
            src_ref=at_tile(send, tgroup * slabs + tslab),
            dst_ref=at_tile(recv, me),
            send_sem=send_sem.at[chunk],
            recv_sem=recv_sem.at[chunk],
            device_id=(tgroup, tslab),
            device_id_type=MESH,
        ).start()

    def keep_own(chunk, from_ref, to_ref, rsems):
        pltpu.make_async_copy(at_block(from_ref, chunk, me), at_block(to_ref, chunk, me), rsems.at[chunk]).start()

    def spread_out(chunk, first):
        def one(step, carry):
            tgroup, tslab = other_of(step)

            @pl.when(tgroup * slabs + tslab != me)
            def _():
                push(chunk, send, recv, send_sem, recv_sem, tgroup, tslab)

            return carry

        lax.fori_loop(first, members, one, 0)
        keep_own(chunk, send, recv, recv_sem)

    def wait_all(ref, sems, chunk):
        pltpu.make_async_copy(ref.at[chunk], ref.at[chunk], sems.at[chunk]).wait()

    def share_planes(step, ref_at, send_at, recv_at):
        tgroup = lax.rem(group + step, groups)
        pltpu.make_async_remote_copy(
            src_ref=ref_at, dst_ref=ref_at, send_sem=send_at, recv_sem=recv_at,
            device_id=(tgroup, slab), device_id_type=MESH,
        ).start()

    for b in range(nbands):
        weights[group, b] = jnp.full((8, 128), occ[b].astype(jnp.float32) * (1.0 / (nbands * groups)))
    loads[1].wait()
    loads[2].wait()
    for tile in range(tiles):
        def start_one(gx, tile=tile):
            prepare(gx, tile)
            z_planes(0, gx, tile, tile + 1)

        if tile == 1:
            loads[3].wait()
        each_gx(start_one)
        if tile == 0:
            pl.semaphore_wait(barrier, members - 1)

        def one(step, carry, tile=tile):
            push_tile(0, tile, *other_of(step))
            return carry

        lax.fori_loop(0, members // 2, one, 0)
    spread_out(0, members // 2)
    for step in range(1, groups):
        share_planes(step, weights.at[group], w_send.at[0], w_recv.at[0])
    for chunk in range(1, chunks):
        each_gx(lambda gx, chunk=chunk: z_planes(chunk, gx, 0, tiles))
        spread_out(chunk, 0)

    others = weights.at[pl.ds(0, groups - 1)]
    pltpu.make_async_copy(others, others, w_recv.at[0]).wait()
    pltpu.make_async_copy(others, others, w_send.at[0]).wait()

    for load in loads[4:]:
        load.wait()

    def middle(chunk, carry):
        wait_all(recv, recv_sem, chunk)
        dens[...] = jnp.zeros_like(dens)

        def build(g, carry):
            arrived = recv[chunk, pl.ds(pl.multiple_of(g * tiles * block, 8), tiles * block), :]
            arrived = arrived.reshape(slabs, tiles, rows, 128)
            high, low = split(
                jnp.concatenate([arrived[:, tile].reshape(block, 128) for tile in range(tiles)], axis=1)
            )
            for b in range(nbands):
                first = b * 128
                lh = high[:, first:first + doubled + 64]
                ll = low[:, first:first + doubled + 64]
                parts = []
                for c in range(2):
                    y = dot(lh, ty[0, b, c]) + dot(lh, ty[1, b, c]) + dot(ll, ty[0, b, c])
                    parts.append(y.reshape(slabs, rows, points))
                w = weights[g, b, 0:1, 0:1]
                for p in range(COUNT):
                    lead = p * (rows - window)
                    stacked = jnp.concatenate(
                        [part[:, lead:lead + window].reshape(slabs * window, points) for part in parts], axis=0
                    )
                    yh, yl = split(stacked)
                    field = dot(tx[0, p], yh) + dot(tx[1, p], yh) + dot(tx[0, p], yl)
                    wave[p, g * nbands + b] = field
                    dens[p] += w * (field[:points] * field[:points] + field[points:] * field[points:])
            return carry

        lax.fori_loop(0, groups, build, 0)
        potentials = []
        for p in range(COUNT):
            d = dens[p]
            outer = ext[:, pl.ds(group * own + chunk * COUNT + p, 1), :].reshape(points, points)
            potential = outer - SLATER * jnp.exp(jnp.log(d) * (1.0 / 3.0))
            potentials.append(potential)
            dens[p] = potential
        place = group * chunks + chunk
        low_rows = pl.ds(pl.multiple_of(place * COUNT * points, 8), COUNT * points)
        high_rows = pl.ds(pl.multiple_of(place * points, 8), points)
        vlow[low_rows, :] = jnp.concatenate([value[:, :128] for value in potentials], axis=0)
        vhigh[high_rows, :] = jnp.concatenate([value[:, 128:] for value in potentials], axis=1)
        for step in range(1, groups):
            share_planes(step, vlow.at[low_rows], v_send.at[0], v_recv.at[0])
            share_planes(step, vhigh.at[high_rows], v_send.at[1], v_recv.at[1])

        def back(turn, carry):
            g = lax.rem(group + turn, groups)
            sums = []
            for b in range(nbands):
                boths = []
                for p in range(COUNT):
                    potential = dens[p]
                    field = wave[p, g * nbands + b]
                    product = jnp.concatenate([field[:points] * potential, field[points:] * potential], axis=0)
                    ph, pll = split(product)
                    boths.append(dot(txb[0, p], ph) + dot(txb[1, p], ph) + dot(txb[0, p], pll))
                total = None
                for c in range(2):
                    low_rows, high_rows = [
                        both[c * slabs * window:(c + 1) * slabs * window].reshape(slabs, window, points) for both in boths
                    ]
                    cut = rows - window
                    merged = jnp.concatenate(
                        [low_rows[:, :cut], low_rows[:, cut:] + high_rows[:, :window - cut], high_rows[:, window - cut:]], axis=1
                    ).reshape(block, points)
                    mh, ml = split(merged)
                    value = dot(mh, tyb[0, b, c]) + dot(mh, tyb[1, b, c]) + dot(ml, tyb[0, b, c])
                    total = value if total is None else total + value
                sums.append(total)
            first, second = sums
            pieces = [first[:, :128], first[:, 128:] + second[:, :128], second[:, 128:]]
            sendb[chunk, pl.ds(pl.multiple_of(g * tiles * block, 8), tiles * block), :] = jnp.concatenate(
                [piece.reshape(slabs, 1, rows, 128) for piece in pieces], axis=1
            ).reshape(tiles * block, 128)

            def one(step, carry):
                tslab = slab_at(step)

                @pl.when(g * slabs + tslab != me)
                def _():
                    push(chunk, sendb, recvb, sendb_sem, recvb_sem, g, tslab)

                return carry

            lax.fori_loop(0, slabs, one, 0)
            return carry

        lax.fori_loop(0, groups, back, 0)
        keep_own(chunk, sendb, recvb, recvb_sem)
        return carry

    lax.fori_loop(0, chunks, middle, 0)

    def z_back(chunk):
        wait_all(recvb, recvb_sem, chunk)

        def one(gx):
            values = z_back_one(recvb, chunk, gx, tzb, chunk, nbands, width, members, rows, planes)
            for b in range(nbands):
                total = values[b]
                if chunk > 0:
                    total = total + out[b, gx]
                if chunk == chunks - 2:
                    index = slab * planes + gx
                    freq = jnp.where(index < width // 2, index, index - width)
                    kinetic = KINETIC * ((freq * freq).astype(jnp.float32) + square[...])
                    total = jnp.where(keep_of(gx), kinetic * coef[b, gx] + total, 0.0)
                out[b, gx] = total

        each_gx(one)

    def wait_planes(sems):
        for place, ref in enumerate((vlow, vhigh)):
            given = ref.at[pl.ds(0, (groups - 1) * (ref.shape[0] // groups))]
            pltpu.make_async_copy(given, given, sems.at[place]).wait()

    for chunk in range(chunks - 1):
        z_back(chunk)

    wait_planes(v_recv)
    spare = points - 128

    def widen(place, carry):
        value = vhigh[pl.ds(pl.multiple_of(place * points, 8), points), :]
        vwide[pl.ds(pl.multiple_of(place * COUNT * points, 8), points), :] = value
        vwide[pl.ds(pl.multiple_of((place * COUNT + 1) * points, 8), points), :] = pltpu.roll(value, spare, 1)
        return carry

    lax.fori_loop(0, groups * chunks, widen, 0)
    layers = own * groups

    def place_row(x, carry):
        first = vlow[pl.ds(x, layers, stride=points), :]
        second = vwide[pl.ds(x, layers, stride=points), :]
        pot[x] = jnp.concatenate([first, second[:, :spare]], axis=1)
        return carry

    lax.fori_loop(0, points, place_row, 0)
    last_table[0] = tzb[chunks - 1]
    wait_all(recvb, recvb_sem, chunks - 1)

    def wait_sent(ref, sems, chunk):
        sent = ref.at[chunk, pl.ds(0, (members - 1) * tiles * rows), :]
        pltpu.make_async_copy(sent, sent, sems.at[chunk]).wait()

    for chunk in range(chunks):
        wait_sent(send, send_sem, chunk)
        wait_sent(sendb, sendb_sem, chunk)
    wait_planes(v_send)


def fused_plan(coefficients, occupation, pencil_reach, external):
    nbands, planes, width, doubled = coefficients.shape
    points = 2 * width
    slabs = lax.axis_size("slab")
    groups = lax.axis_size("band")
    layers = points // slabs
    own = layers // groups
    chunks = own // COUNT
    members = groups * slabs
    rows = COUNT * planes
    lanes = nbands * doubled
    first, *rest, last = fused_tables(width, nbands, planes, slabs, groups, own)
    tables = [jnp.asarray(np.concatenate(split_np(first), axis=1))]
    tables += [jnp.asarray(np.stack(split_np(table))) for table in rest]
    high, low = split_np(last)
    tables += [jnp.asarray(np.concatenate([high, low, high], axis=2))]
    wavenumbers = np.where(np.arange(width) < width // 2, np.arange(width), np.arange(width) - width)
    twice = np.concatenate([wavenumbers, wavenumbers])
    square = jnp.asarray((wavenumbers[:, None] ** 2 + twice[None] ** 2).astype(np.float32))
    vmem = pl.BlockSpec(memory_space=pltpu.VMEM)
    smem = pl.BlockSpec(memory_space=pltpu.SMEM)
    hbm = pl.BlockSpec(memory_space=pl.ANY)
    operands = [coefficients, pencil_reach, occupation, external, square] + tables
    bf, f32 = jnp.bfloat16, jnp.float32
    dma = pltpu.SemaphoreType.DMA
    exchange = pltpu.VMEM((chunks, members * rows * lanes // 128, 128), f32)
    mixed = pltpu.VMEM((planes, nbands * 2 * width, doubled), bf)
    results = [
        pltpu.VMEM(coefficients.shape, f32),
        pltpu.VMEM(external.shape, f32),
        exchange,
        pltpu.VMEM((planes, width, 128), f32),
        pltpu.VMEM((1,) + tables[-1].shape[1:], bf),
    ]
    gathered = pl.pallas_call(
        functools.partial(fused_kernel, (nbands, planes, width, slabs, groups, own)),
        name="fused",
        out_shape=results,
        in_specs=[hbm, hbm, smem, hbm, hbm] + [hbm] * len(tables),
        out_specs=[vmem] * len(results),
        scratch_shapes=[
            pltpu.VMEM(coefficients.shape, f32),
            pltpu.VMEM(pencil_reach.shape, jnp.int32),
            pltpu.VMEM(external.shape, f32),
            pltpu.VMEM(square.shape, f32),
        ] + [pltpu.VMEM(table.shape, bf) for table in tables] + [
            mixed, mixed, exchange, exchange, exchange,
            pltpu.VMEM((COUNT, groups * nbands, 2 * points, points), f32),
            pltpu.VMEM((COUNT, points, points), f32),
            pltpu.VMEM((groups, nbands, 8, 128), f32),
            pltpu.VMEM((layers * points, 128), f32),
            pltpu.VMEM((groups * chunks * points, 128), f32),
            pltpu.VMEM((layers * points, 128), f32),
            dma((11,)), dma((chunks,)), dma((chunks,)), dma((chunks,)), dma((chunks,)),
            dma((2,)), dma((2,)), dma((1,)), dma((1,)),
        ],
        compiler_params=pltpu.CompilerParams(
            collective_id=0, has_side_effects=True, vmem_limit_bytes=46 * 2**20
        ),
    )(*operands)
    return pl.pallas_call(
        functools.partial(finish_kernel, (nbands, planes, width, members)),
        name="finish",
        out_shape=[
            jax.ShapeDtypeStruct(coefficients.shape, f32),
            jax.ShapeDtypeStruct(external.shape, f32),
        ],
        in_specs=[vmem] * len(results),
        out_specs=[hbm, hbm],
        scratch_shapes=[pltpu.VMEM(coefficients.shape, f32), dma, dma],
        compiler_params=pltpu.CompilerParams(vmem_limit_bytes=12 * 2**20),
    )(*gathered)


def shards(coefficients, occupation, pencil_reach, external):
    nbands, planes, width, doubled = coefficients.shape
    slabs, groups = lax.axis_size("slab"), lax.axis_size("band")
    layers = doubled // slabs
    fits = (
        layers % (groups * COUNT) == 0 and layers > groups * COUNT and nbands == 2 and planes == 12 and width == 96 and slabs % 2 == 0
    )
    plan = fused_plan if fits else slab_plan
    return plan(coefficients, occupation, pencil_reach, external)


def solution(mesh):
    return jax.shard_map(
        shards,
        mesh=mesh,
        in_specs=(P("band", "slab", None, None), P("band"), P("slab", None), P(None, "slab", None)),
        out_specs=(P("band", "slab", None, None), P(None, "slab", None)),
        check_vma=False,
    )
```

```python
import functools
import math

import jax
import jax.numpy as jnp
import ml_dtypes
import numpy as np
from jax import lax
from jax.experimental import pallas as pl
from jax.experimental.pallas import tpu as pltpu
from jax.sharding import PartitionSpec as P

KINETIC = 0.0005
SLATER = 0.9847
COUNT = 2
UNROLL = 3
MESH = pl.DeviceIdType.MESH


def frequency(length):
    indices = jnp.arange(length, dtype=jnp.int32)
    return jnp.where(indices < length // 2, indices, indices - length)


def inverse_table(length, extent):
    wavenumbers = frequency(length)
    positions = jnp.arange(extent, dtype=jnp.int32)
    phases = positions[:, None] * wavenumbers[None, :] % extent
    angles = phases.astype(jnp.float32) * (2.0 * math.pi / extent)
    factor = length ** (-0.5)
    cosine = jnp.cos(angles) * factor
    sine_part = jnp.sin(angles) * factor
    return jnp.stack([jnp.stack([cosine, -sine_part], 1), jnp.stack([sine_part, cosine], 1)], 0)


def forward_table(length, extent):
    wavenumbers = frequency(length)
    positions = jnp.arange(extent, dtype=jnp.int32)
    phases = wavenumbers[:, None] * positions[None, :] % extent
    angles = phases.astype(jnp.float32) * (2.0 * math.pi / extent)
    factor = length**0.5 / extent
    cosine = jnp.cos(angles) * factor
    sine_part = jnp.sin(angles) * factor
    return jnp.stack([jnp.stack([cosine, sine_part], 1), jnp.stack([-sine_part, cosine], 1)], 0)


def contract(form, left, right):
    return jnp.einsum(form, left, right, precision=lax.Precision.HIGH)


def slab_plan(coefficients, occupation, pencil_reach, external):
    nbands, planes, width, doubled = coefficients.shape
    points = 2 * width
    slabs = lax.axis_size("slab")
    layers = points // slabs
    groups = lax.axis_size("band")
    inverse = inverse_table(width, points)
    forward = forward_table(width, points)
    wavenumbers = frequency(width)
    sphere = (jnp.abs(wavenumbers)[None, None, :] <= pencil_reach[:, :, None]).astype(jnp.float32)
    sphere_full = sphere[None, :, :, None, :]
    masked = coefficients.reshape(nbands, planes, width, 2, width) * sphere_full
    along_z = contract("bxgci,onci->bxnog", masked, inverse)
    flattened = along_z.reshape(nbands, planes, points, 2 * width)
    received = lax.all_to_all(flattened, "slab", split_axis=2, concat_axis=1, tiled=True)
    columns = received.reshape(received.shape[0], width, layers, 2, width)
    spread = contract("bkzcg,oycg->bkzoy", columns, inverse)
    wavefield = contract("bkzcy,oxck->bxzoy", spread, inverse)
    squares = jnp.sum(wavefield * wavefield, axis=3)
    weights = occupation.astype(jnp.float32) / (nbands * groups)
    partial_value = contract("b,bxzy->xzy", weights, squares)
    rows_all = points * layers
    share = (rows_all + groups - 1) // groups
    flat_partial = partial_value.reshape(rows_all, points)
    density = lax.psum_scatter(flat_partial, "band", scatter_dimension=0, tiled=True)
    flat_external = external.reshape(rows_all, points)
    start_row = lax.axis_index("band") * share
    own_external = lax.dynamic_slice_in_dim(flat_external, start_row, share, 0)
    own_potential = own_external - SLATER * jnp.cbrt(density)
    gathered = lax.all_gather(own_potential, "band", axis=0, tiled=True)
    potential_all = gathered.reshape(points, layers, points)
    product = wavefield * potential_all[None, :, :, None, :]
    back_rows = contract("bxzcy,okcx->bkzoy", product, forward)
    back_y = contract("bkzcy,ogcy->bkzog", back_rows, forward).reshape(
        nbands, width, layers, 2 * width
    )
    received = lax.all_to_all(back_y, "slab", split_axis=1, concat_axis=2, tiled=True)
    blocks = received.reshape(received.shape[0], planes, points, 2, width)
    returned = contract("bxncg,ohcn->bxgoh", blocks, forward)
    plane_index = lax.axis_index("slab") * planes + jnp.arange(planes, dtype=jnp.int32)
    plane_freq = jnp.where(plane_index < width // 2, plane_index, plane_index - width)
    plane_sq = (plane_freq * plane_freq).astype(jnp.float32)
    wave_sq = (wavenumbers * wavenumbers).astype(jnp.float32)
    kinetic = KINETIC * (plane_sq[:, None, None] + wave_sq[None, :, None] + wave_sq[None, None, :])
    finished = sphere_full * (kinetic[None, :, :, None, :] * masked + returned)
    return (finished.reshape(nbands, planes, width, 2 * width), potential_all)


def split_np(table):
    high = table.astype(ml_dtypes.bfloat16)
    low = (table - high.astype(np.float64)).astype(ml_dtypes.bfloat16)
    return high, low


def split(value):
    high = value.astype(jnp.bfloat16)
    low = (value - high.astype(jnp.float32)).astype(jnp.bfloat16)
    return high, low


def dot(left, right):
    return jnp.dot(left, right, preferred_element_type=jnp.float32)


def dot_t(left, right):
    return lax.dot_general(left, right, (((1,), (1,)), ((), ())), preferred_element_type=jnp.float32)


def fused_tables(width, nbands, planes, slabs, groups, own):
    points = 2 * width
    doubled = 2 * width
    layers = points // slabs
    chunks = own // COUNT
    rows = COUNT * planes
    indices = np.arange(width)
    wave = np.where(indices < width // 2, indices, indices - width)
    phase = (np.arange(points)[:, None] * wave[None, :]) % points
    angles = phase * (2.0 * math.pi / points)
    cos, sin = np.cos(angles), np.sin(angles)
    inv = width**-0.5
    fwd = width**0.5 / points
    z_of = np.array(
        [
            [
                s * layers + g * own + part * COUNT + p
                for p in range(COUNT)
                for g in range(groups)
                for s in range(slabs)
            ]
            for part in range(chunks)
        ]
    )
    tz = np.concatenate([cos, -sin], 1)[z_of] * inv
    span = doubled + 64
    ty = np.zeros((nbands, 2, span, points))
    tyb = np.zeros((nbands, 2, points, span))
    for b in range(nbands):
        shift = b * doubled - b * 128
        ty[b, 0, shift:shift + width] = cos.T * inv
        ty[b, 0, shift + width:shift + doubled] = -sin.T * inv
        ty[b, 1, shift:shift + width] = sin.T * inv
        ty[b, 1, shift + width:shift + doubled] = cos.T * inv
        tyb[b, 0, :, shift:shift + width] = cos * fwd
        tyb[b, 0, :, shift + width:shift + doubled] = -sin * fwd
        tyb[b, 1, :, shift:shift + width] = sin * fwd
        tyb[b, 1, :, shift + width:shift + doubled] = cos * fwd
    window = 16
    tx = np.zeros((COUNT, 2, points, 2, slabs, window))
    txb = np.zeros((COUNT, 2, slabs, window, 2, points))
    for p in range(COUNT):
        first = p * planes - p * (rows - window)
        put = slice(first, first + planes)
        c3 = cos.reshape(points, slabs, planes)
        s3 = sin.reshape(points, slabs, planes)
        tx[p, 0, :, 0][:, :, put] = c3 * inv
        tx[p, 0, :, 1][:, :, put] = -s3 * inv
        tx[p, 1, :, 0][:, :, put] = s3 * inv
        tx[p, 1, :, 1][:, :, put] = c3 * inv
        ct, st = c3.transpose(1, 2, 0), s3.transpose(1, 2, 0)
        txb[p, 0][:, put, 0] = ct * fwd
        txb[p, 0][:, put, 1] = st * fwd
        txb[p, 1][:, put, 0] = -st * fwd
        txb[p, 1][:, put, 1] = ct * fwd
    tx = tx.reshape(COUNT, 2 * points, 2 * slabs * window)
    txb = txb.reshape(COUNT, 2 * slabs * window, 2 * points)
    tzb = np.stack([np.concatenate([cos, -sin], 1)[z_of], np.concatenate([sin, cos], 1)[z_of]], 1) * fwd
    return tz, ty, tx, txb, tyb, tzb


def keep_rows(column, gx, width):
    lane = lax.rem(lax.broadcasted_iota(jnp.int32, (1, 2 * width), 1), width)
    absk = jnp.where(lane < width // 2, lane, width - lane).astype(jnp.float32)
    return absk <= column[gx][:, 0:1]


def z_back_one(landed, chunk, gx, table, part, nbands, width, members, rows, planes):
    tiles = nbands * 2 * width // 128
    columns = []
    for tile in range(tiles):
        starts = [tile * rows + p * planes + gx for p in range(COUNT)]
        columns.append(jnp.concatenate(
            [landed[chunk, pl.ds(start, members, stride=tiles * rows), :] for start in starts], axis=0
        ))
    high, low = split(jnp.concatenate(columns, axis=1))
    turned = jnp.concatenate([high, high, low], axis=0).T
    values = []
    for b in range(nbands):
        total = None
        for c in range(2):
            first = (b * 2 + c) * width
            part_sum = dot(turned[first:first + width], table[part, c])
            total = part_sum if total is None else total + part_sum
        values.append(total)
    return values


def finish_kernel(sizes, start, pot, landed, column, table, out_hbm, pot_hbm, out, out_sem, pot_sem):
    nbands, planes, width, members = sizes
    whole = pltpu.make_async_copy(pot, pot_hbm, pot_sem)
    whole.start()
    chunk = landed.shape[0] - 1

    def some(turn, carry):
        for gx in [turn * UNROLL + place for place in range(UNROLL)]:
            values = z_back_one(landed, chunk, gx, table, 0, nbands, width, members, COUNT * planes, planes)
            for b in range(nbands):
                out[b, gx] = start[b, gx] + jnp.where(keep_rows(column, gx, width), values[b], 0.0)
                pltpu.make_async_copy(out.at[b, gx], out_hbm.at[b, gx], out_sem).start()
        return carry

    lax.fori_loop(0, planes // UNROLL, some, 0)
    pltpu.make_async_copy(out, out_hbm, out_sem).wait()
    whole.wait()


def fused_kernel(
    sizes,
    coef_hbm, reach_hbm, occ, ext_hbm, square_hbm, tz_hbm, ty_hbm, tx_hbm, txb_hbm, tyb_hbm, tzb_hbm,
    out, pot, recvb, column, last_table,
    coef, reach, ext, square, tz, ty, tx, txb, tyb, tzb,
    xh, xl, send, recv, sendb, wave, dens, weights, vlow, vhigh, vwide,
    load_sem, send_sem, recv_sem, sendb_sem, recvb_sem, v_send, v_recv, w_send, w_recv,
):
    nbands, planes, width, slabs, groups, own = sizes
    points = 2 * width
    doubled = 2 * width
    chunks = own // COUNT
    members = groups * slabs
    rows = COUNT * planes
    block = slabs * rows
    tiles = nbands * doubled // 128
    window = 16
    zs = COUNT * members
    group = lax.axis_index("band")
    slab = lax.axis_index("slab")
    me = group * slabs + slab

    def at_block(ref, chunk, member):
        return ref.at[chunk, pl.ds(pl.multiple_of(member * tiles * rows, 8), tiles * rows), :]

    loads = [
        pltpu.make_async_copy(source, target, load_sem.at[place])
        for place, (source, target) in enumerate([
            (reach_hbm, reach), (tz_hbm, tz), (coef_hbm, coef),
            (ty_hbm, ty), (tx_hbm, tx), (ext_hbm, ext), (txb_hbm, txb), (tyb_hbm, tyb), (tzb_hbm, tzb),
            (square_hbm, square),
        ])
    ]
    for load in loads:
        load.start()

    barrier = pltpu.get_barrier_semaphore()

    def greet(step, carry):
        other = lax.rem(me + step, members)
        pl.semaphore_signal(barrier, inc=1, device_id=(other // slabs, lax.rem(other, slabs)), device_id_type=MESH)
        return carry

    lax.fori_loop(1, members, greet, 0)

    loads[0].wait()
    turned_reach = reach[...].astype(jnp.float32).T
    for gx in range(planes):
        column[gx] = jnp.broadcast_to(turned_reach[:, gx:gx + 1], (width, 128))

    def keep_of(gx):
        return keep_rows(column, gx, width)

    def prepare(gx, b):
        value = jnp.where(keep_of(gx), coef[b, gx], 0.0)
        turned = jnp.concatenate([value[:, width:], -value[:, :width]], axis=1)
        high, low = split(jnp.concatenate([value, turned], axis=0))
        xh[gx, b * doubled:(b + 1) * doubled] = high
        xl[gx, b * doubled:(b + 1) * doubled] = low

    def z_planes(chunk, gx, first_tile, last_tile):
        lanes = slice(first_tile * 128, last_tile * 128)
        both = dot_t(tz[chunk], xh[gx, lanes])
        value = both[:zs] + both[zs:] + dot_t(tz[chunk, :zs], xl[gx, lanes])
        for p in range(COUNT):
            for tile in range(first_tile, last_tile):
                start = tile * rows + p * planes + gx
                place = tile - first_tile
                piece = value[p * members:(p + 1) * members, place * 128:(place + 1) * 128]
                send[chunk, pl.ds(start, members, stride=tiles * rows), :] = piece

    def each_gx(work):
        def some(turn, carry):
            for place in range(UNROLL):
                work(turn * UNROLL + place)
            return carry

        lax.fori_loop(0, planes // UNROLL, some, 0)

    half = slabs // 2

    def slab_at(turn):
        side = lax.rem(slab // half + 1 + turn // half, 2)
        return side * half + lax.rem(slab + turn, half)

    def other_of(step):
        return lax.rem(group + lax.rem(step, groups), groups), slab_at(step // groups)

    def push(chunk, from_ref, to_ref, sems, rsems, tgroup, tslab):
        pltpu.make_async_remote_copy(
            src_ref=at_block(from_ref, chunk, tgroup * slabs + tslab),
            dst_ref=at_block(to_ref, chunk, me),
            send_sem=sems.at[chunk],
            recv_sem=rsems.at[chunk],
            device_id=(tgroup, tslab),
            device_id_type=MESH,
        ).start()

    def push_tiles(chunk, first, last, tgroup, tslab):
        def at_tiles(ref, member):
            start = pl.multiple_of((member * tiles + first) * rows, 8)
            return ref.at[chunk, pl.ds(start, (last - first) * rows), :]

        pltpu.make_async_remote_copy(
            src_ref=at_tiles(send, tgroup * slabs + tslab),
            dst_ref=at_tiles(recv, me),
            send_sem=send_sem.at[chunk],
            recv_sem=recv_sem.at[chunk],
            device_id=(tgroup, tslab),
            device_id_type=MESH,
        ).start()

    def keep_own(chunk, from_ref, to_ref, rsems):
        pltpu.make_async_copy(at_block(from_ref, chunk, me), at_block(to_ref, chunk, me), rsems.at[chunk]).start()

    def spread_out(chunk, first):
        def one(step, carry):
            tgroup, tslab = other_of(step)

            @pl.when(tgroup * slabs + tslab != me)
            def _():
                push(chunk, send, recv, send_sem, recv_sem, tgroup, tslab)

            return carry

        lax.fori_loop(first, members, one, 0)
        keep_own(chunk, send, recv, recv_sem)

    def wait_all(ref, sems, chunk):
        pltpu.make_async_copy(ref.at[chunk], ref.at[chunk], sems.at[chunk]).wait()

    def share_planes(step, ref_at, send_at, recv_at):
        tgroup = lax.rem(group + step, groups)
        pltpu.make_async_remote_copy(
            src_ref=ref_at, dst_ref=ref_at, send_sem=send_at, recv_sem=recv_at,
            device_id=(tgroup, slab), device_id_type=MESH,
        ).start()

    for b in range(nbands):
        weights[group, b] = jnp.full((8, 128), occ[b].astype(jnp.float32) * (1.0 / (nbands * groups)))
    loads[1].wait()
    loads[2].wait()
    for first, last in ((0, 1), (1, tiles)):
        def start_one(gx, first=first, last=last):
            prepare(gx, first)
            z_planes(0, gx, first, last)

        each_gx(start_one)
        if first == 0:
            pl.semaphore_wait(barrier, members - 1)

        def one(step, carry, first=first, last=last):
            push_tiles(0, first, last, *other_of(step))
            return carry

        lax.fori_loop(0, members // 2, one, 0)
    spread_out(0, members // 2)
    for step in range(1, groups):
        share_planes(step, weights.at[group], w_send.at[0], w_recv.at[0])
    for chunk in range(1, chunks):
        each_gx(lambda gx, chunk=chunk: z_planes(chunk, gx, 0, tiles))
        spread_out(chunk, 0)

    others = weights.at[pl.ds(0, groups - 1)]
    pltpu.make_async_copy(others, others, w_recv.at[0]).wait()
    pltpu.make_async_copy(others, others, w_send.at[0]).wait()

    for load in loads[3:]:
        load.wait()

    def middle(chunk, carry):
        wait_all(recv, recv_sem, chunk)
        dens[...] = jnp.zeros_like(dens)

        def build(g, carry):
            arrived = recv[chunk, pl.ds(pl.multiple_of(g * tiles * block, 8), tiles * block), :]
            arrived = arrived.reshape(slabs, tiles, rows, 128)
            high, low = split(
                jnp.concatenate([arrived[:, tile].reshape(block, 128) for tile in range(tiles)], axis=1)
            )
            for b in range(nbands):
                first = b * 128
                lh = high[:, first:first + doubled + 64]
                ll = low[:, first:first + doubled + 64]
                parts = []
                for c in range(2):
                    y = dot(lh, ty[0, b, c]) + dot(lh, ty[1, b, c]) + dot(ll, ty[0, b, c])
                    parts.append(y.reshape(slabs, rows, points))
                w = weights[g, b, 0:1, 0:1]
                for p in range(COUNT):
                    lead = p * (rows - window)
                    stacked = jnp.concatenate(
                        [part[:, lead:lead + window].reshape(slabs * window, points) for part in parts], axis=0
                    )
                    yh, yl = split(stacked)
                    field = dot(tx[0, p], yh) + dot(tx[1, p], yh) + dot(tx[0, p], yl)
                    wave[p, g * nbands + b] = field
                    dens[p] += w * (field[:points] * field[:points] + field[points:] * field[points:])
            return carry

        lax.fori_loop(0, groups, build, 0)
        potentials = []
        for p in range(COUNT):
            d = dens[p]
            outer = ext[:, pl.ds(group * own + chunk * COUNT + p, 1), :].reshape(points, points)
            potential = outer - SLATER * jnp.exp(jnp.log(d) * (1.0 / 3.0))
            potentials.append(potential)
            dens[p] = potential
        place = group * chunks + chunk
        low_rows = pl.ds(pl.multiple_of(place * COUNT * points, 8), COUNT * points)
        high_rows = pl.ds(pl.multiple_of(place * points, 8), points)
        vlow[low_rows, :] = jnp.concatenate([value[:, :128] for value in potentials], axis=0)
        vhigh[high_rows, :] = jnp.concatenate([value[:, 128:] for value in potentials], axis=1)
        for step in range(1, groups):
            share_planes(step, vlow.at[low_rows], v_send.at[0], v_recv.at[0])
            share_planes(step, vhigh.at[high_rows], v_send.at[1], v_recv.at[1])

        def back(turn, carry):
            g = lax.rem(group + turn, groups)
            sums = []
            for b in range(nbands):
                boths = []
                for p in range(COUNT):
                    potential = dens[p]
                    field = wave[p, g * nbands + b]
                    product = jnp.concatenate([field[:points] * potential, field[points:] * potential], axis=0)
                    ph, pll = split(product)
                    boths.append(dot(txb[0, p], ph) + dot(txb[1, p], ph) + dot(txb[0, p], pll))
                total = None
                for c in range(2):
                    low_rows, high_rows = [
                        both[c * slabs * window:(c + 1) * slabs * window].reshape(slabs, window, points) for both in boths
                    ]
                    cut = rows - window
                    merged = jnp.concatenate(
                        [low_rows[:, :cut], low_rows[:, cut:] + high_rows[:, :window - cut], high_rows[:, window - cut:]], axis=1
                    ).reshape(block, points)
                    mh, ml = split(merged)
                    value = dot(mh, tyb[0, b, c]) + dot(mh, tyb[1, b, c]) + dot(ml, tyb[0, b, c])
                    total = value if total is None else total + value
                sums.append(total)
            first, second = sums
            pieces = [first[:, :128], first[:, 128:] + second[:, :128], second[:, 128:]]
            sendb[chunk, pl.ds(pl.multiple_of(g * tiles * block, 8), tiles * block), :] = jnp.concatenate(
                [piece.reshape(slabs, 1, rows, 128) for piece in pieces], axis=1
            ).reshape(tiles * block, 128)

            def one(step, carry):
                tslab = slab_at(step)

                @pl.when(g * slabs + tslab != me)
                def _():
                    push(chunk, sendb, recvb, sendb_sem, recvb_sem, g, tslab)

                return carry

            lax.fori_loop(0, slabs, one, 0)
            return carry

        lax.fori_loop(0, groups, back, 0)
        keep_own(chunk, sendb, recvb, recvb_sem)
        return carry

    lax.fori_loop(0, chunks, middle, 0)

    def z_back(chunk):
        wait_all(recvb, recvb_sem, chunk)

        def one(gx):
            values = z_back_one(recvb, chunk, gx, tzb, chunk, nbands, width, members, rows, planes)
            for b in range(nbands):
                total = values[b]
                if chunk > 0:
                    total = total + out[b, gx]
                if chunk == chunks - 2:
                    index = slab * planes + gx
                    freq = jnp.where(index < width // 2, index, index - width)
                    kinetic = KINETIC * ((freq * freq).astype(jnp.float32) + square[...])
                    total = jnp.where(keep_of(gx), kinetic * coef[b, gx] + total, 0.0)
                out[b, gx] = total

        each_gx(one)

    def wait_planes(sems):
        for place, ref in enumerate((vlow, vhigh)):
            given = ref.at[pl.ds(0, (groups - 1) * (ref.shape[0] // groups))]
            pltpu.make_async_copy(given, given, sems.at[place]).wait()

    for chunk in range(chunks - 1):
        z_back(chunk)

    wait_planes(v_recv)
    spare = points - 128

    def widen(place, carry):
        value = vhigh[pl.ds(pl.multiple_of(place * points, 8), points), :]
        vwide[pl.ds(pl.multiple_of(place * COUNT * points, 8), points), :] = value
        vwide[pl.ds(pl.multiple_of((place * COUNT + 1) * points, 8), points), :] = pltpu.roll(value, spare, 1)
        return carry

    lax.fori_loop(0, groups * chunks, widen, 0)
    layers = own * groups

    def place_row(x, carry):
        first = vlow[pl.ds(x, layers, stride=points), :]
        second = vwide[pl.ds(x, layers, stride=points), :]
        pot[x] = jnp.concatenate([first, second[:, :spare]], axis=1)
        return carry

    lax.fori_loop(0, points, place_row, 0)
    last_table[0] = tzb[chunks - 1]
    wait_all(recvb, recvb_sem, chunks - 1)

    def wait_sent(ref, sems, chunk):
        sent = ref.at[chunk, pl.ds(0, (members - 1) * tiles * rows), :]
        pltpu.make_async_copy(sent, sent, sems.at[chunk]).wait()

    for chunk in range(chunks):
        wait_sent(send, send_sem, chunk)
        wait_sent(sendb, sendb_sem, chunk)
    wait_planes(v_send)


def fused_plan(coefficients, occupation, pencil_reach, external):
    nbands, planes, width, doubled = coefficients.shape
    points = 2 * width
    slabs = lax.axis_size("slab")
    groups = lax.axis_size("band")
    layers = points // slabs
    own = layers // groups
    chunks = own // COUNT
    members = groups * slabs
    rows = COUNT * planes
    lanes = nbands * doubled
    first, *rest, last = fused_tables(width, nbands, planes, slabs, groups, own)
    tables = [jnp.asarray(np.concatenate(split_np(first), axis=1))]
    tables += [jnp.asarray(np.stack(split_np(table))) for table in rest]
    high, low = split_np(last)
    tables += [jnp.asarray(np.concatenate([high, low, high], axis=2))]
    wavenumbers = np.where(np.arange(width) < width // 2, np.arange(width), np.arange(width) - width)
    twice = np.concatenate([wavenumbers, wavenumbers])
    square = jnp.asarray((wavenumbers[:, None] ** 2 + twice[None] ** 2).astype(np.float32))
    vmem = pl.BlockSpec(memory_space=pltpu.VMEM)
    smem = pl.BlockSpec(memory_space=pltpu.SMEM)
    hbm = pl.BlockSpec(memory_space=pl.ANY)
    operands = [coefficients, pencil_reach, occupation, external, square] + tables
    bf, f32 = jnp.bfloat16, jnp.float32
    dma = pltpu.SemaphoreType.DMA
    exchange = pltpu.VMEM((chunks, members * rows * lanes // 128, 128), f32)
    mixed = pltpu.VMEM((planes, nbands * 2 * width, doubled), bf)
    results = [
        pltpu.VMEM(coefficients.shape, f32),
        pltpu.VMEM(external.shape, f32),
        exchange,
        pltpu.VMEM((planes, width, 128), f32),
        pltpu.VMEM((1,) + tables[-1].shape[1:], bf),
    ]
    gathered = pl.pallas_call(
        functools.partial(fused_kernel, (nbands, planes, width, slabs, groups, own)),
        name="fused",
        out_shape=results,
        in_specs=[hbm, hbm, smem, hbm, hbm] + [hbm] * len(tables),
        out_specs=[vmem] * len(results),
        scratch_shapes=[
            pltpu.VMEM(coefficients.shape, f32),
            pltpu.VMEM(pencil_reach.shape, jnp.int32),
            pltpu.VMEM(external.shape, f32),
            pltpu.VMEM(square.shape, f32),
        ] + [pltpu.VMEM(table.shape, bf) for table in tables] + [
            mixed, mixed, exchange, exchange, exchange,
            pltpu.VMEM((COUNT, groups * nbands, 2 * points, points), f32),
            pltpu.VMEM((COUNT, points, points), f32),
            pltpu.VMEM((groups, nbands, 8, 128), f32),
            pltpu.VMEM((layers * points, 128), f32),
            pltpu.VMEM((groups * chunks * points, 128), f32),
            pltpu.VMEM((layers * points, 128), f32),
            dma((10,)), dma((chunks,)), dma((chunks,)), dma((chunks,)), dma((chunks,)),
            dma((2,)), dma((2,)), dma((1,)), dma((1,)),
        ],
        compiler_params=pltpu.CompilerParams(
            collective_id=0, has_side_effects=True, vmem_limit_bytes=46 * 2**20
        ),
    )(*operands)
    return pl.pallas_call(
        functools.partial(finish_kernel, (nbands, planes, width, members)),
        name="finish",
        out_shape=[
            jax.ShapeDtypeStruct(coefficients.shape, f32),
            jax.ShapeDtypeStruct(external.shape, f32),
        ],
        in_specs=[vmem] * len(results),
        out_specs=[hbm, hbm],
        scratch_shapes=[pltpu.VMEM(coefficients.shape, f32), dma, dma],
        compiler_params=pltpu.CompilerParams(vmem_limit_bytes=12 * 2**20),
    )(*gathered)


def shards(coefficients, occupation, pencil_reach, external):
    nbands, planes, width, doubled = coefficients.shape
    slabs, groups = lax.axis_size("slab"), lax.axis_size("band")
    layers = doubled // slabs
    fits = (
        layers % (groups * COUNT) == 0 and layers > groups * COUNT and nbands == 2 and planes == 12 and width == 96 and slabs % 2 == 0
    )
    plan = fused_plan if fits else slab_plan
    return plan(coefficients, occupation, pencil_reach, external)


def solution(mesh):
    return jax.shard_map(
        shards,
        mesh=mesh,
        in_specs=(P("band", "slab", None, None), P("band"), P("slab", None), P(None, "slab", None)),
        out_specs=(P("band", "slab", None, None), P(None, "slab", None)),
        check_vma=False,
    )
```
